256 devices in a mesh: ens: 2 (over z_hi), tile: 128 (over x, y, z_lo, core).
Axes of the slice: x: 4, y: 4, z: 8 (z_hi: 2, z_lo: 4; z = z_hi * 4 + z_lo), core: 2. Of those that a mesh axis runs over, the one named last changes fastest.
Arguments:
- fields: bfloat16 [2, 128, 48, 48, 128], P('ens', 'tile'), may hold values from -6 to 6
- weight_first: bfloat16 [3, 3, 128, 128], replicated, may hold values from -0.1875 to 0.1875
- weight_second: bfloat16 [3, 3, 128, 128], replicated, may hold values from -0.1875 to 0.1875
- neighbours: int32 [128, 4], replicated, may hold values from 0 to 127, as said below
- cotangent: bfloat16 [2, 128, 48, 48, 128], P('ens', 'tile'), may hold values from -6 to 6
Outputs:
- out_field: bfloat16 [2, 128, 48, 48, 128], P('ens', 'tile')
- grad_fields: bfloat16 [2, 128, 48, 48, 128], P('ens', 'tile')
- grad_first: float32 [3, 3, 128, 128], replicated
- grad_second: float32 [3, 3, 128, 128], replicated
The draws below stay inside these ranges and needn't reach their ends.
Inputs may be any that keep to these rules, and one draw needn't show every extreme that they name: The tiles form a grid of 8 rows of 16: the tile at index p has the four neighbours p - 16, p + 1, p + 16 and p - 1 modulo 128, one beside each side, listed clockwise from a starting side that varies from tile to tile; the relation is mutual.
All inputs are finite; a program needn't handle non-finite values.
Results may differ from the reference program's by a relative error of at most 0.0061.
Values may be sent and summed in bfloat16 or wider, within the bound.
A program may use at most 64 MiB of HBM per device.

```python
import jax
import jax.numpy as jnp
from jax import lax

C = 128
S = 48
ENS = 2
NT = 128
COLS = 16


def draw_neighbours(key, part):
    turns = jax.random.randint(key, (NT,), 0, 4)
    offsets = jnp.array([-COLS, 1, COLS, -1], jnp.int32)
    sides = jnp.arange(4, dtype=jnp.int32)
    global_side = (sides[None, :] + turns[:, None]) % 4
    tiles = jnp.arange(NT, dtype=jnp.int32)[:, None]
    return ((tiles + offsets[global_side]) % NT).astype(jnp.int32)


def levels(own_key, shape, pieces, low, high):
    factor_of, own = 1.0, jax.random.fold_in(own_key, 6)
    for axis_at, blocks in pieces:
        steps = jnp.exp(jax.random.uniform(jax.random.fold_in(own, axis_at), (blocks,), jnp.float32, low / len(pieces), high / len(pieces)))
        factor_of = factor_of * jnp.repeat(steps, shape[axis_at] // blocks).reshape([-1 if axis == axis_at else 1 for axis in range(len(shape))])
    return factor_of


def normal_values(key, shape, spread, reach, cuts=(), held_as=jnp.bfloat16):
    level = levels(key, shape, cuts, -0.22, 0.18) if cuts else 1.0
    result = jax.random.normal(key, shape, jnp.float32) * spread * level
    return jnp.minimum(jnp.maximum(result, -reach), reach).astype(held_as)


def setup_inputs(seed: int = 0) -> dict:
    key_of = jax.random.split(jax.random.key(seed), 6)
    fields = normal_values(key_of[0], (ENS, NT, S, S, C), 1.0, 6.0, ((0, 2), (1, 128)))
    weight_first = normal_values(key_of[1], (3, 3, C, C), (9 * C) ** -0.5, 0.1875)
    weight_second = normal_values(key_of[2], (3, 3, C, C), (9 * C) ** -0.5, 0.1875)
    neighbours = draw_neighbours(jax.random.fold_in(key_of[5], 71), 0)
    cotangent = normal_values(key_of[4], (ENS, NT, S, S, C), 1.0, 6.0, ((0, 2), (1, 128)))
    return {"fields": fields, "weight_first": weight_first, "weight_second": weight_second, "neighbours": neighbours, "cotangent": cotangent}


root_half = 0.7071067811865476
inv_root_tau = 0.3989422804014327

def gelu_value(pre):
    return 0.5 * pre * (1.0 + lax.erf(pre * root_half))

def gelu_slope(pre):
    return 0.5 * (1.0 + lax.erf(pre * root_half)) + pre * jnp.exp(-0.5 * pre * pre) * inv_root_tau

def strips(block):
    top_row = block[..., 0, :, :]
    right_col = block[..., :, -1, :]
    bottom_row = block[..., -1, ::-1, :]
    left_col = block[..., ::-1, 0, :]
    return jnp.stack([top_row, right_col, bottom_row, left_col], axis=-3)

def assemble(block, halo_strips):
    top_row = halo_strips[..., 0, :, :]
    right_col = halo_strips[..., 1, :, :]
    bottom_row = halo_strips[..., 2, ::-1, :]
    left_col = halo_strips[..., 3, ::-1, :]
    corner_nw = 0.5 * (top_row[..., 0, :] + left_col[..., 0, :])
    corner_ne = 0.5 * (top_row[..., -1, :] + right_col[..., 0, :])
    corner_sw = 0.5 * (left_col[..., -1, :] + bottom_row[..., 0, :])
    corner_se = 0.5 * (bottom_row[..., -1, :] + right_col[..., -1, :])
    first_row = jnp.concatenate([corner_nw[..., None, :], top_row, corner_ne[..., None, :]], axis=-2)
    last_row = jnp.concatenate([corner_sw[..., None, :], bottom_row, corner_se[..., None, :]], axis=-2)
    middle = jnp.concatenate([left_col[..., :, None, :], block, right_col[..., :, None, :]], axis=-2)
    return jnp.concatenate([first_row[..., None, :, :], middle, last_row[..., None, :, :]], axis=-3)

def convolve(padded, weight):
    extent = padded.shape[-2] - 2
    accumulated = 0.0
    for a in range(3):
        for b in range(3):
            window = padded[..., a:a + extent, b:b + extent, :].reshape(-1, padded.shape[-1])
            accumulated = accumulated + jnp.dot(window, weight[a, b], preferred_element_type=jnp.float32)
    return accumulated.reshape(padded.shape[:-3] + (extent, extent, weight.shape[-1]))

def weight_grad(padded, delta):
    extent = delta.shape[-2]
    flat_delta = delta.reshape(-1, delta.shape[-1])
    tap_rows = []
    for a in range(3):
        tap_cols = []
        for b in range(3):
            window = padded[..., a:a + extent, b:b + extent, :].reshape(-1, padded.shape[-1])
            tap_cols.append(jnp.dot(window.T, flat_delta, preferred_element_type=jnp.float32))
        tap_rows.append(jnp.stack(tap_cols))
    return jnp.stack(tap_rows)

def convolve_back(delta, weight):
    flat_delta = delta.reshape(-1, delta.shape[-1])
    accumulated = 0.0
    for a in range(3):
        for b in range(3):
            term = jnp.dot(flat_delta, weight[a, b].T, preferred_element_type=jnp.float32)
            term = term.reshape(delta.shape[:-1] + (weight.shape[-2],))
            widths = [(0, 0)] * (delta.ndim - 3) + [(a, 2 - a), (b, 2 - b), (0, 0)]
            accumulated = accumulated + jnp.pad(term, widths)
    return accumulated

def pull_whole(own_strips, neighbours, facing):
    return own_strips[neighbours, facing][:, :, ::-1, :]

def forward_layer(block, weight, neighbours, facing):
    halo_strips = pull_whole(strips(block), neighbours, facing)
    padded = assemble(block.astype(jnp.float32), halo_strips.astype(jnp.float32)).astype(jnp.bfloat16)
    return (padded, halo_strips, convolve(padded, weight))

def backward_layer(block, halo_strips, delta, weight, neighbours, facing):
    grad_padded = convolve_back(delta, weight)
    unused, adjoint = jax.vjp(assemble, block.astype(jnp.float32), halo_strips.astype(jnp.float32))
    grad_block, grad_halo = adjoint(grad_padded)
    returned = pull_whole(grad_halo.astype(jnp.bfloat16), neighbours, facing)
    unused_two, strip_adjoint = jax.vjp(strips, block.astype(jnp.float32))
    rim_term, = strip_adjoint(returned.astype(jnp.float32))
    return grad_block + rim_term

def reference(fields, weight_first, weight_second, neighbours, cotangent):
    back_links = neighbours[neighbours]
    matches = back_links == jnp.arange(NT, dtype=jnp.int32)[:, None, None]
    facing = lax.optimization_barrier(jnp.sum(jnp.where(matches, jnp.arange(4, dtype=jnp.int32)[None, None, :], 0), axis=-1)).astype(jnp.int32)
    outputs = []
    grads = []
    grad_first = jnp.zeros((3, 3, C, C), jnp.float32)
    grad_second = jnp.zeros((3, 3, C, C), jnp.float32)
    for m in range(ENS):
        block = fields[m]
        padded_one, halo_one, first_pre = forward_layer(block, weight_first, neighbours, facing)
        hidden = gelu_value(first_pre).astype(jnp.bfloat16)
        padded_two, halo_two, second_pre = forward_layer(hidden, weight_second, neighbours, facing)
        outputs.append(gelu_value(second_pre).astype(jnp.bfloat16))
        delta_second = (cotangent[m].astype(jnp.float32) * gelu_slope(second_pre)).astype(jnp.bfloat16)
        grad_second = grad_second + weight_grad(padded_two, delta_second)
        grad_hidden = backward_layer(hidden, halo_two, delta_second, weight_second, neighbours, facing)
        delta_first = (grad_hidden * gelu_slope(first_pre)).astype(jnp.bfloat16)
        grad_first = grad_first + weight_grad(padded_one, delta_first)
        grad_block = backward_layer(block, halo_one, delta_first, weight_first, neighbours, facing)
        grads.append(grad_block.astype(jnp.bfloat16))
    return (jnp.stack(outputs), jnp.stack(grads), grad_first, grad_second)
```

```python
import jax
import jax.numpy as jnp
from jax import lax
from jax.experimental import pallas as pl
from jax.experimental.pallas import tpu as pltpu
from jax.sharding import PartitionSpec as P

MESH = pl.DeviceIdType.MESH
root_half = 0.7071067811865476
inv_root_tau = 0.3989422804014327


def from_behind(block, axis, distance):
    devices = range(lax.axis_size(axis))
    route = [((i - distance) % len(devices), i) for i in devices]
    return lax.ppermute(block, axis, route)


def gelu_value(pre):
    return 0.5 * pre * (1.0 + lax.erf(pre * root_half))


def gelu_slope(pre):
    return 0.5 * (1.0 + lax.erf(pre * root_half)) + pre * jnp.exp(-0.5 * pre * pre) * inv_root_tau


def strips(block):
    top_row = block[..., 0, :, :]
    right_col = block[..., :, -1, :]
    bottom_row = block[..., -1, ::-1, :]
    left_col = block[..., ::-1, 0, :]
    return jnp.stack([top_row, right_col, bottom_row, left_col], axis=-3)


def assemble(block, halo_strips):
    top_row = halo_strips[..., 0, :, :]
    right_col = halo_strips[..., 1, :, :]
    bottom_row = halo_strips[..., 2, ::-1, :]
    left_col = halo_strips[..., 3, ::-1, :]
    corner_nw = 0.5 * (top_row[..., 0, :] + left_col[..., 0, :])
    corner_ne = 0.5 * (top_row[..., -1, :] + right_col[..., 0, :])
    corner_sw = 0.5 * (left_col[..., -1, :] + bottom_row[..., 0, :])
    corner_se = 0.5 * (bottom_row[..., -1, :] + right_col[..., -1, :])
    first_row = jnp.concatenate(
        [corner_nw[..., None, :], top_row, corner_ne[..., None, :]], axis=-2
    )
    last_row = jnp.concatenate(
        [corner_sw[..., None, :], bottom_row, corner_se[..., None, :]], axis=-2
    )
    middle = jnp.concatenate(
        [left_col[..., :, None, :], block, right_col[..., :, None, :]], axis=-2
    )
    return jnp.concatenate([first_row[..., None, :, :], middle, last_row[..., None, :, :]], axis=-3)


def convolve(padded, weight):
    extent = padded.shape[-2] - 2
    accumulated = 0.0
    for a in range(3):
        for b in range(3):
            window = padded[..., a : a + extent, b : b + extent, :].reshape(-1, padded.shape[-1])
            accumulated = accumulated + jnp.dot(
                window, weight[a, b], preferred_element_type=jnp.float32
            )
    return accumulated.reshape(padded.shape[:-3] + (extent, extent, weight.shape[-1]))


def weight_grad(padded, delta):
    extent = delta.shape[-2]
    flat_delta = delta.reshape(-1, delta.shape[-1])
    tap_rows = []
    for a in range(3):
        tap_cols = []
        for b in range(3):
            window = padded[..., a : a + extent, b : b + extent, :].reshape(-1, padded.shape[-1])
            tap_cols.append(jnp.dot(window.T, flat_delta, preferred_element_type=jnp.float32))
        tap_rows.append(jnp.stack(tap_cols))
    return jnp.stack(tap_rows)


def convolve_back(delta, weight):
    flat_delta = delta.reshape(-1, delta.shape[-1])
    accumulated = 0.0
    for a in range(3):
        for b in range(3):
            term = jnp.dot(flat_delta, weight[a, b].T, preferred_element_type=jnp.float32)
            term = term.reshape(delta.shape[:-1] + (weight.shape[-2],))
            widths = [(0, 0)] * (delta.ndim - 3) + [(a, 2 - a), (b, 2 - b), (0, 0)]
            accumulated = accumulated + jnp.pad(term, widths)
    return accumulated


def pull_strips(own_strips, neighbours, returning):
    tile_index = lax.axis_index("tile")
    tile_count = lax.axis_size("tile")
    row_length = max(4, tile_count // 8)
    offsets = [1, -1, row_length, -row_length]
    own_links = lax.dynamic_slice(neighbours, (tile_index, 0), (1, 4))[0]
    relative = (own_links - tile_index) % tile_count
    strip_width = own_strips.shape[1] * own_strips.shape[2]
    flattened = own_strips.reshape(4, strip_width)
    received = []
    for offset in offsets:
        if returning:
            bundle = from_behind(flattened, "tile", -offset)
        else:
            bundle = from_behind(flattened, "tile", -offset)
        sender = (tile_index + offset) % tile_count
        sender_links = lax.dynamic_slice(neighbours, (sender, 0), (1, 4))
        choose_side = (sender_links == tile_index).astype(jnp.bfloat16)
        incoming = jnp.dot(choose_side, bundle, preferred_element_type=jnp.float32).astype(
            jnp.bfloat16
        )
        received.append(incoming)
    stacked = jnp.concatenate(received, axis=0)
    targets = jnp.array([offset % tile_count for offset in offsets], jnp.int32)
    direction_hit = (relative[:, None] == targets[None, :]).astype(jnp.bfloat16)
    halo_strips = jnp.dot(direction_hit, stacked, preferred_element_type=jnp.float32).astype(
        jnp.bfloat16
    )
    return halo_strips.reshape(own_strips.shape)[:, ::-1, :]


def forward_layer(block, weight, neighbours):
    halo_strips = pull_strips(strips(block), neighbours, False)
    padded = assemble(block.astype(jnp.float32), halo_strips.astype(jnp.float32)).astype(
        jnp.bfloat16
    )
    return (padded, halo_strips, convolve(padded, weight))


def backward_layer(block, halo_strips, delta, weight, neighbours):
    grad_padded = convolve_back(delta, weight)
    unused, adjoint = jax.vjp(assemble, block.astype(jnp.float32), halo_strips.astype(jnp.float32))
    grad_block, grad_halo = adjoint(grad_padded)
    returned = pull_strips(grad_halo.astype(jnp.bfloat16), neighbours, True)
    unused_two, strip_adjoint = jax.vjp(strips, block.astype(jnp.float32))
    (rim_term,) = strip_adjoint(returned.astype(jnp.float32))
    return grad_block + rim_term


TAPS = 5


class Place:
    def __init__(self):
        ens = lax.axis_index("ens")
        tile = lax.axis_index("tile")
        self.tile = tile
        self.core = tile % 2
        self.z = ens * 4 + (tile // 2) % 4
        self.q = tile // 8

    def device(self, q, z, core):
        return {"ens": z // 4, "tile": q * 8 + (z % 4) * 2 + core}


def greet(me):
    barrier = pltpu.get_barrier_semaphore()

    def signal(target):
        pl.semaphore_signal(barrier, inc=1, device_id=target, device_id_type=MESH)

    def plane(r, carry):
        signal(me.device((me.q + r) % 16, me.z, me.core))
        signal(me.device((me.q + r) % 16, me.z, 1 - me.core))
        return carry

    signal(me.device(me.q, me.z, 1 - me.core))
    lax.fori_loop(1, 16, plane, 0)

    def column(r, carry):
        signal(me.device(me.q, (me.z + r) % 8, me.core))
        return carry

    lax.fori_loop(1, 8, column, 0)
    return barrier


class Reduce:
    def __init__(self, me, grad, pair_out, pair_in, part, plane_in, column_in, whole, sems):
        self.me, self.grad = me, grad
        self.pair_out, self.pair_in, self.part = pair_out, pair_in, part
        self.plane_in, self.column_in, self.whole = plane_in, column_in, whole
        self.sems = sems

    def pair_copy(self):
        me = self.me
        return pltpu.make_async_remote_copy(
            src_ref=self.pair_out,
            dst_ref=self.pair_in,
            send_sem=self.sems.at[0, 0],
            recv_sem=self.sems.at[1, 0],
            device_id=me.device(me.q, me.z, 1 - me.core),
            device_id_type=MESH,
        )

    def plane_copy(self, target, source):
        return pltpu.make_async_remote_copy(
            src_ref=self.part.at[target],
            dst_ref=self.plane_in.at[source],
            send_sem=self.sems.at[0, 1 + target],
            recv_sem=self.sems.at[1, 1 + source],
            device_id=self.me.device(target, self.me.z, self.me.core),
            device_id_type=MESH,
        )

    def column_copy(self, target, source):
        return pltpu.make_async_remote_copy(
            src_ref=self.column_in.at[source],
            dst_ref=self.column_in.at[source],
            send_sem=self.sems.at[0, 17 + target],
            recv_sem=self.sems.at[1, 17 + source],
            device_id=self.me.device(self.me.q, target, self.me.core),
            device_id_type=MESH,
        )

    def whole_copy(self, target, target_core, source, source_core):
        return pltpu.make_async_remote_copy(
            src_ref=self.whole.at[source_core, source],
            dst_ref=self.whole.at[source_core, source],
            send_sem=self.sems.at[0, 25 + 16 * target_core + target],
            recv_sem=self.sems.at[1, 25 + 16 * source_core + source],
            device_id=self.me.device(target, self.me.z, target_core),
            device_id_type=MESH,
        )

    def send_pair(self):
        other = 1 - self.me.core
        for t in range(TAPS):
            self.pair_out[t] = self.grad[4 * other + t].astype(jnp.bfloat16)
        self.pair_copy().start()

    def send_plane(self):
        me = self.me
        self.pair_copy().wait_recv()

        def band(m, carry):
            rows = pl.ds(pl.multiple_of(16 * m, 16), 16)
            for t in range(TAPS):
                total = self.grad[4 * me.core + t, rows, :] + self.pair_in[t, rows, :].astype(
                    jnp.float32
                )
                self.part[2 * m, t] = total[:8].astype(jnp.bfloat16)
                self.part[2 * m + 1, t] = total[8:].astype(jnp.bfloat16)
            return carry

        lax.fori_loop(0, 8, band, 0)
        self.plane_in[me.q] = self.part[me.q]

        def send(r, carry):
            self.plane_copy((me.q + r) % 16, me.q).start()
            return carry

        lax.fori_loop(1, 16, send, 0)

    def send_column(self):
        me = self.me

        def wait(r, carry):
            self.plane_copy((me.q + r) % 16, (me.q + r) % 16).wait_recv()
            return carry

        lax.fori_loop(1, 16, wait, 0)
        for t in range(TAPS):
            total = self.plane_in[0, t].astype(jnp.float32)
            for k in range(1, 16):
                total = total + self.plane_in[k, t].astype(jnp.float32)
            self.column_in[me.z, t] = total.astype(jnp.bfloat16)

        def send(r, carry):
            self.column_copy((me.z + r) % 8, me.z).start()
            return carry

        lax.fori_loop(1, 8, send, 0)

    def send_whole(self):
        me = self.me

        def wait(r, carry):
            self.column_copy((me.z + r) % 8, (me.z + r) % 8).wait_recv()
            return carry

        lax.fori_loop(1, 8, wait, 0)
        for t in range(TAPS):
            total = self.column_in[0, t].astype(jnp.float32)
            for k in range(1, 8):
                total = total + self.column_in[k, t].astype(jnp.float32)
            self.whole[me.core, me.q, t] = total.astype(jnp.bfloat16)

        def send(r, carry):
            target = (me.q + r) % 16
            self.whole_copy(target, me.core, me.q, me.core).start()
            self.whole_copy(target, 1 - me.core, me.q, me.core).start()
            return carry

        self.whole_copy(me.q, 1 - me.core, me.q, me.core).start()
        lax.fori_loop(1, 16, send, 0)

    def finish(self, out):
        me = self.me

        def wait(r, carry):
            source = (me.q + r) % 16
            self.whole_copy(source, me.core, source, me.core).wait_recv()
            self.whole_copy(source, 1 - me.core, source, 1 - me.core).wait_recv()
            return carry

        self.whole_copy(me.q, 1 - me.core, me.q, 1 - me.core).wait_recv()
        lax.fori_loop(1, 16, wait, 0)
        for tap in range(9):
            core = 0 if tap < TAPS else 1
            for k in range(16):
                out[tap, 8 * k : 8 * k + 8, :] = self.whole[core, k, tap - 4 * core].astype(
                    jnp.float32
                )

    def drain(self):
        me = self.me
        self.pair_copy().wait_send()

        def plane(r, carry):
            target = (me.q + r) % 16
            self.plane_copy(target, me.q).wait_send()
            self.whole_copy(target, me.core, me.q, me.core).wait_send()
            self.whole_copy(target, 1 - me.core, me.q, me.core).wait_send()
            return carry

        lax.fori_loop(1, 16, plane, 0)
        self.whole_copy(me.q, 1 - me.core, me.q, me.core).wait_send()

        def column(r, carry):
            self.column_copy((me.z + r) % 8, me.z).wait_send()
            return carry

        lax.fori_loop(1, 8, column, 0)


REDUCE_SCRATCH = [
    pltpu.VMEM((TAPS, 128, 128), jnp.bfloat16),
    pltpu.VMEM((TAPS, 128, 128), jnp.bfloat16),
    pltpu.VMEM((16, TAPS, 8, 128), jnp.bfloat16),
    pltpu.VMEM((16, TAPS, 8, 128), jnp.bfloat16),
    pltpu.VMEM((8, TAPS, 8, 128), jnp.bfloat16),
    pltpu.VMEM((2, 16, TAPS, 8, 128), jnp.bfloat16),
    pltpu.SemaphoreType.DMA((2, 57)),
]


def reduce_kernel(first, second, first_out, second_out, *scratch):
    me = Place()
    barrier = greet(me)
    pl.semaphore_wait(barrier, 38)
    half = len(REDUCE_SCRATCH)
    jobs = [Reduce(me, second, *scratch[:half]), Reduce(me, first, *scratch[half:])]
    for job in jobs:
        job.send_pair()
    for job in jobs:
        job.send_plane()
    for job in jobs:
        job.send_column()
    for job in jobs:
        job.send_whole()
    jobs[0].finish(second_out)
    jobs[1].finish(first_out)
    for job in jobs:
        job.drain()


def reduce_everywhere(first, second):
    vmem = pl.BlockSpec(memory_space=pltpu.VMEM)
    shape = jax.ShapeDtypeStruct((9, 128, 128), jnp.float32)
    first, second = pl.pallas_call(
        reduce_kernel,
        out_shape=(shape, shape),
        in_specs=[vmem, vmem],
        out_specs=(vmem, vmem),
        scratch_shapes=REDUCE_SCRATCH + REDUCE_SCRATCH,
        compiler_params=pltpu.CompilerParams(collective_id=0, has_side_effects=True),
    )(first.reshape(9, 128, 128), second.reshape(9, 128, 128))
    return first.reshape(3, 3, 128, 128), second.reshape(3, 3, 128, 128)


def local(fields, weight_first, weight_second, neighbours, cotangent):
    block = fields[0, 0]
    padded_one, halo_one, first_pre = forward_layer(block, weight_first, neighbours)
    hidden = gelu_value(first_pre).astype(jnp.bfloat16)
    padded_two, halo_two, second_pre = forward_layer(hidden, weight_second, neighbours)
    out_field = gelu_value(second_pre).astype(jnp.bfloat16)
    delta_second = (cotangent[0, 0].astype(jnp.float32) * gelu_slope(second_pre)).astype(
        jnp.bfloat16
    )
    grad_second = weight_grad(padded_two, delta_second)
    grad_hidden = backward_layer(hidden, halo_two, delta_second, weight_second, neighbours)
    delta_first = (grad_hidden * gelu_slope(first_pre)).astype(jnp.bfloat16)
    grad_first = weight_grad(padded_one, delta_first)
    grad_block = backward_layer(block, halo_one, delta_first, weight_first, neighbours)
    grad_first, grad_second = reduce_everywhere(grad_first, grad_second)
    return (
        out_field[None, None],
        grad_block.astype(jnp.bfloat16)[None, None],
        grad_first,
        grad_second,
    )


def solution(mesh):
    placed = (P("ens", "tile", None, None, None), P(), P(), P(), P("ens", "tile", None, None, None))
    return jax.shard_map(
        local,
        mesh=mesh,
        in_specs=placed,
        out_specs=(
            P("ens", "tile", None, None, None),
            P("ens", "tile", None, None, None),
            P(),
            P(),
        ),
        check_vma=False,
    )
```

```python
import jax
import jax.numpy as jnp
from jax import lax
from jax.experimental import pallas as pl
from jax.experimental.pallas import tpu as pltpu
from jax.sharding import PartitionSpec as P

MESH = pl.DeviceIdType.MESH
root_half = 0.7071067811865476
inv_root_tau = 0.3989422804014327
f32, bf16 = jnp.float32, jnp.bfloat16
S, C = 48, 128
PITCH = 64
SLOT = 64
OFFSETS = (1, -1, 16, -16)


TAPS = 5


class Place:
    def __init__(self):
        ens = lax.axis_index("ens")
        tile = lax.axis_index("tile")
        self.tile = tile
        self.core = tile % 2
        self.z = ens * 4 + (tile // 2) % 4
        self.q = tile // 8

    def device(self, q, z, core):
        return {"ens": z // 4, "tile": q * 8 + (z % 4) * 2 + core}


def greet(me):
    barrier = pltpu.get_barrier_semaphore()

    def signal(target):
        pl.semaphore_signal(barrier, inc=1, device_id=target, device_id_type=MESH)

    def plane(r, carry):
        signal(me.device((me.q + r) % 16, me.z, me.core))
        signal(me.device((me.q + r) % 16, me.z, 1 - me.core))
        return carry

    signal(me.device(me.q, me.z, 1 - me.core))
    lax.fori_loop(1, 16, plane, 0)

    def column(r, carry):
        signal(me.device(me.q, (me.z + r) % 8, me.core))
        return carry

    lax.fori_loop(1, 8, column, 0)
    for step in (1, -1):
        signal({"tile": (me.tile + step) % 128})
    return barrier


class Reduce:
    def __init__(self, me, grad, pair_out, pair_in, part, plane_in, column_in, whole, sems):
        self.me, self.grad = me, grad
        self.pair_out, self.pair_in, self.part = pair_out, pair_in, part
        self.plane_in, self.column_in, self.whole = plane_in, column_in, whole
        self.sems = sems

    def pair_copy(self):
        me = self.me
        return pltpu.make_async_remote_copy(
            src_ref=self.pair_out,
            dst_ref=self.pair_in,
            send_sem=self.sems.at[0, 0],
            recv_sem=self.sems.at[1, 0],
            device_id=me.device(me.q, me.z, 1 - me.core),
            device_id_type=MESH,
        )

    def plane_copy(self, target, source):
        return pltpu.make_async_remote_copy(
            src_ref=self.part.at[target],
            dst_ref=self.plane_in.at[source],
            send_sem=self.sems.at[0, 1 + target],
            recv_sem=self.sems.at[1, 1 + source],
            device_id=self.me.device(target, self.me.z, self.me.core),
            device_id_type=MESH,
        )

    def column_copy(self, target, source):
        return pltpu.make_async_remote_copy(
            src_ref=self.column_in.at[source],
            dst_ref=self.column_in.at[source],
            send_sem=self.sems.at[0, 17 + target],
            recv_sem=self.sems.at[1, 17 + source],
            device_id=self.me.device(self.me.q, target, self.me.core),
            device_id_type=MESH,
        )

    def whole_copy(self, target, target_core, source, source_core):
        return pltpu.make_async_remote_copy(
            src_ref=self.whole.at[source_core, source],
            dst_ref=self.whole.at[source_core, source],
            send_sem=self.sems.at[0, 25 + 16 * target_core + target],
            recv_sem=self.sems.at[1, 25 + 16 * source_core + source],
            device_id=self.me.device(target, self.me.z, target_core),
            device_id_type=MESH,
        )

    def send_pair(self):
        other = 1 - self.me.core
        for t in range(TAPS):
            self.pair_out[t] = self.grad[4 * other + t].astype(bf16)
        self.pair_copy().start()

    def send_plane(self):
        me = self.me
        self.pair_copy().wait_recv()

        def band(m, carry):
            rows = pl.ds(pl.multiple_of(16 * m, 16), 16)
            for t in range(TAPS):
                total = self.grad[4 * me.core + t, rows, :] + self.pair_in[t, rows, :].astype(f32)
                self.part[2 * m, t] = total[:8].astype(bf16)
                self.part[2 * m + 1, t] = total[8:].astype(bf16)
            return carry

        lax.fori_loop(0, 8, band, 0)
        self.plane_in[me.q] = self.part[me.q]

        def send(r, carry):
            self.plane_copy((me.q + r) % 16, me.q).start()
            return carry

        lax.fori_loop(1, 16, send, 0)

    def send_column(self):
        me = self.me

        def wait(r, carry):
            self.plane_copy((me.q + r) % 16, (me.q + r) % 16).wait_recv()
            return carry

        lax.fori_loop(1, 16, wait, 0)
        for t in range(TAPS):
            total = self.plane_in[0, t].astype(f32)
            for k in range(1, 16):
                total = total + self.plane_in[k, t].astype(f32)
            self.column_in[me.z, t] = total.astype(bf16)

        def send(r, carry):
            self.column_copy((me.z + r) % 8, me.z).start()
            return carry

        lax.fori_loop(1, 8, send, 0)

    def send_whole(self):
        me = self.me

        def wait(r, carry):
            self.column_copy((me.z + r) % 8, (me.z + r) % 8).wait_recv()
            return carry

        lax.fori_loop(1, 8, wait, 0)
        for t in range(TAPS):
            total = self.column_in[0, t].astype(f32)
            for k in range(1, 8):
                total = total + self.column_in[k, t].astype(f32)
            self.whole[me.core, me.q, t] = total.astype(bf16)

        def send(r, carry):
            target = (me.q + r) % 16
            self.whole_copy(target, me.core, me.q, me.core).start()
            self.whole_copy(target, 1 - me.core, me.q, me.core).start()
            return carry

        self.whole_copy(me.q, 1 - me.core, me.q, me.core).start()
        lax.fori_loop(1, 16, send, 0)

    def finish(self, out):
        me = self.me

        def wait(r, carry):
            source = (me.q + r) % 16
            self.whole_copy(source, me.core, source, me.core).wait_recv()
            self.whole_copy(source, 1 - me.core, source, 1 - me.core).wait_recv()
            return carry

        self.whole_copy(me.q, 1 - me.core, me.q, 1 - me.core).wait_recv()
        lax.fori_loop(1, 16, wait, 0)
        for tap in range(9):
            core = 0 if tap < TAPS else 1
            for k in range(16):
                out[tap, 8 * k : 8 * k + 8, :] = self.whole[core, k, tap - 4 * core].astype(
                    f32
                )

    def drain(self):
        me = self.me
        self.pair_copy().wait_send()

        def plane(r, carry):
            target = (me.q + r) % 16
            self.plane_copy(target, me.q).wait_send()
            self.whole_copy(target, me.core, me.q, me.core).wait_send()
            self.whole_copy(target, 1 - me.core, me.q, me.core).wait_send()
            return carry

        lax.fori_loop(1, 16, plane, 0)
        self.whole_copy(me.q, 1 - me.core, me.q, me.core).wait_send()

        def column(r, carry):
            self.column_copy((me.z + r) % 8, me.z).wait_send()
            return carry

        lax.fori_loop(1, 8, column, 0)


REDUCE_SCRATCH = [
    pltpu.VMEM((TAPS, 128, 128), bf16),
    pltpu.VMEM((TAPS, 128, 128), bf16),
    pltpu.VMEM((16, TAPS, 8, 128), bf16),
    pltpu.VMEM((16, TAPS, 8, 128), bf16),
    pltpu.VMEM((8, TAPS, 8, 128), bf16),
    pltpu.VMEM((2, 16, TAPS, 8, 128), bf16),
    pltpu.SemaphoreType.DMA((2, 57)),
]


class Swap:
    def __init__(self, me, outgoing, incoming, sems):
        self.me, self.outgoing, self.incoming, self.sems = me, outgoing, incoming, sems

    def copy(self, d):
        return pltpu.make_async_remote_copy(
            src_ref=self.outgoing.at[d, pl.ds(0, S)],
            dst_ref=self.incoming.at[d ^ 1, pl.ds(0, S)],
            send_sem=self.sems.at[0, d],
            recv_sem=self.sems.at[1, d ^ 1],
            device_id={"tile": (self.me.tile + OFFSETS[d]) % 128},
            device_id_type=MESH,
        )

    def send(self, strips, choose):
        routed = jnp.dot(choose[...], strips, preferred_element_type=f32).astype(bf16)
        for d in range(4):
            self.outgoing[d] = routed[SLOT * d : SLOT * d + SLOT]
        for d in range(4):
            self.copy(d).start()

    def receive(self, place):
        for d in range(4):
            self.copy(d).wait_recv()
        return jnp.dot(
            place[...], self.incoming[...].reshape(4 * SLOT, C), preferred_element_type=f32
        )

    def drain(self):
        for d in range(4):
            self.copy(d).wait_send()


def routing(me, neighbours, choose, place):
    sides = []
    for offset in OFFSETS:
        target = (me.tile + offset) % 128
        side = jnp.int32(0)
        for s in range(1, 4):
            side = side + jnp.where(neighbours[me.tile, s] == target, s, 0)
        sides.append(side)
    row = lax.broadcasted_iota(jnp.int32, (256, 256), 0)
    col = lax.broadcasted_iota(jnp.int32, (256, 256), 1)
    i, j = row % SLOT, col % SLOT
    inside = (i < S) & (j < S)
    same, flip = inside & (i == j), inside & (i + j == S - 1)

    def side_of(direction):
        out = jnp.full((256, 256), sides[0], jnp.int32)
        for d in range(1, 4):
            out = jnp.where(direction == d, sides[d], out)
        return out

    side = col // SLOT
    hit = (side_of(row // SLOT) == side) & (((side < 2) & same) | ((side >= 2) & flip))
    choose[...] = jnp.where(hit, 1.0, 0.0).astype(bf16)
    side = row // SLOT
    hit = (side_of(col // SLOT) == side) & (((side < 2) & flip) | ((side >= 2) & same))
    place[...] = jnp.where(hit, 1.0, 0.0).astype(bf16)


def edge_strips(padded, base):
    fill = jnp.zeros((SLOT - S, C), f32)

    def row(i):
        return padded[pl.ds(PITCH * (i + base) + 8, S), :]

    def column(j):
        return padded[pl.ds(PITCH * base + 8 + j, S, stride=PITCH), :]

    parts = []
    for strip in (row(0), column(S - 1), row(S - 1), column(0)):
        parts += [strip, fill]
    return jnp.concatenate(parts, axis=0).astype(bf16)


def spread(padded, base, wide, first, count):
    view = padded.reshape(padded.shape[0] // PITCH, PITCH, C)

    def body(k, carry):
        r = first + k
        for b in range(3):
            wide[r, :, C * b : C * b + C] = view[r + base, pl.ds(7 + b, S), :].astype(bf16)
        return carry

    lax.fori_loop(0, count, body, 0, unroll=4)


def fill_halo(padded, halo, wide):
    top, right, bottom, left = (halo[SLOT * s : SLOT * s + S] for s in range(4))
    padded[pl.ds(PITCH + 7, S, stride=PITCH), :] = left
    padded[pl.ds(PITCH + 56, S, stride=PITCH), :] = right
    padded[pl.ds(8, S), :] = top
    padded[pl.ds(PITCH * 49 + 8, S), :] = bottom
    padded[pl.ds(7, 1), :] = 0.5 * (top[:1] + left[:1])
    padded[pl.ds(56, 1), :] = 0.5 * (top[S - 1 :] + right[:1])
    padded[pl.ds(PITCH * 49 + 7, 1), :] = 0.5 * (left[S - 1 :] + bottom[:1])
    padded[pl.ds(PITCH * 49 + 56, 1), :] = 0.5 * (bottom[S - 1 :] + right[S - 1 :])
    view = padded.reshape(50, PITCH, C)
    for r in (0, 49):
        for b in range(3):
            wide[r, :, C * b : C * b + C] = view[r, pl.ds(7 + b, S), :].astype(bf16)

    def body(k, carry):
        r = 1 + k
        wide[r, :16, :C] = view[r, pl.ds(7, 16), :].astype(bf16)
        wide[r, 32:, 2 * C :] = view[r, pl.ds(41, 16), :].astype(bf16)
        return carry

    lax.fori_loop(0, S, body, 0, unroll=4)


def taps_of(wide, start):
    return jnp.concatenate(
        [wide[pl.ds(start + a, 8)].reshape(8 * S, 3 * C) for a in range(3)], axis=1
    )


def dot_rows(rows, weight):
    return lax.dot_general(rows, weight, (((1,), (1,)), ((), ())), preferred_element_type=f32)


def halo_gradients(delta, turned):
    fill = jnp.zeros((SLOT - S, C), f32)
    index = lax.broadcasted_iota(jnp.int32, (S, C), 0)

    def along_row(i):
        return [delta[pl.ds(PITCH * (i + 2) + 6 + t, 56), :] for t in range(3)]

    def along_column(j):
        return [delta[pl.ds(PITCH * t + 8 + j, 56, stride=PITCH), :] for t in range(3)]

    def block(a, b):
        return turned[:, C * (3 * a + b) : C * (3 * a + b) + C]

    sides = (
        (along_row(0), [block(2, t) for t in range(3)]),
        (along_column(S - 1), [block(t, 0) for t in range(3)]),
        (along_row(S - 1), [block(0, t) for t in range(3)]),
        (along_column(0), [block(t, 2) for t in range(3)]),
    )
    parts = []
    for lines, blocks in sides:
        full = dot_rows(
            jnp.concatenate(lines, axis=1).astype(bf16), jnp.concatenate(blocks, axis=1)
        )
        strip = full[1 : S + 1]
        strip = strip + jnp.where(index == 0, 0.5 * full[:1], 0.0)
        strip = strip + jnp.where(index == S - 1, 0.5 * full[S + 1 : S + 2], 0.0)
        parts += [strip, fill]
    return jnp.concatenate(parts, axis=0).astype(bf16)


def turn(weight, turned):
    for k in range(9):
        turned[:, C * k : C * k + C] = weight[8 - k]


def weight_gradient(delta, delta_t, wide, grad):
    view = delta.reshape(delta.shape[0] // PITCH, PITCH, C)
    for k in range(6):
        rows = view[pl.ds(2 + 8 * k, 8), pl.ds(8, S), :].reshape(8 * S, C)
        delta_t[:, 8 * S * k : 8 * S * (k + 1)] = rows.T.astype(bf16)

    def body(a, carry):
        flat = wide[pl.ds(a, S)].reshape(S * S, 3 * C)
        product = jnp.dot(delta_t[...], flat, preferred_element_type=f32)
        for b in range(3):
            grad[3 * a + b] = product[:, C * b : C * b + C].T
        return carry

    lax.fori_loop(0, 3, body, 0)


def field_gradient(wide, turned, grad):
    def body(k, carry):
        rows = pl.ds(pl.multiple_of(8 * S * k, 8 * S), 8 * S)
        grad[rows, :] = dot_rows(taps_of(wide, 8 * k), turned[...])
        return carry

    lax.fori_loop(0, 6, body, 0)


def add_strips(grad, strips):
    top, right, bottom, left = (strips[SLOT * s : SLOT * s + S] for s in range(4))
    grad[pl.ds(0, S), :] += top
    grad[pl.ds(S * (S - 1), S), :] += bottom
    grad[pl.ds(0, S, stride=S), :] += left
    grad[pl.ds(S - 1, S, stride=S), :] += right


def step_kernel(
    fields, weight_first, weight_second, neighbours, cotangent,
    out_field, grad_fields, first_out, second_out,
    padded, delta, wide_first, wide_second, wide_delta, delta_t, slope, grad,
    turned_first, turned_second, choose, place, outgoing, incoming, swap_sems,
    grad_first, grad_second, *reduce_scratch,
):
    me = Place()
    barrier = greet(me)
    half = len(REDUCE_SCRATCH)
    second_sum = Reduce(me, grad_second, *reduce_scratch[:half])
    first_sum = Reduce(me, grad_first, *reduce_scratch[half:])
    swaps = [Swap(me, outgoing.at[e], incoming.at[e], swap_sems.at[e]) for e in range(4)]

    routing(me, neighbours, choose, place)
    incoming[:, :, S:, :] = jnp.zeros((4, 4, SLOT - S, C), bf16)
    padded_view = padded.reshape(50, PITCH, C)
    delta_view = delta.reshape(58, PITCH, C)
    for r in (0, 1, 50, 51, 52, 53, 54, 55, 56, 57):
        delta_view[r] = jnp.zeros((PITCH, C), f32)
    delta_view[2:50, :8, :] = jnp.zeros((S, 8, C), f32)
    delta_view[2:50, 56:, :] = jnp.zeros((S, 8, C), f32)

    def load(k, carry):
        padded_view[pl.ds(1 + 8 * k, 8), pl.ds(8, S), :] = fields[pl.ds(8 * k, 8)].astype(f32)
        return carry

    lax.fori_loop(0, 6, load, 0)
    strips = edge_strips(padded, 1)
    pl.semaphore_wait(barrier, 40)
    swaps[0].send(strips, choose)
    spread(padded, 0, wide_first, 1, S)
    turn(weight_first, turned_first)
    turn(weight_second, turned_second)
    fill_halo(padded, swaps[0].receive(place), wide_first)

    def forward_first(k, carry):
        pre = jnp.dot(
            taps_of(wide_first, 8 * k),
            weight_first[...].reshape(9 * C, C),
            preferred_element_type=f32,
        )
        below = 0.5 * (1.0 + lax.erf(pre * root_half))
        rows = pl.ds(pl.multiple_of(8 * S * k, 8 * S), 8 * S)
        slope[rows, :] = below + pre * jnp.exp(-0.5 * pre * pre) * inv_root_tau
        hidden = (pre * below).astype(bf16).astype(f32)
        padded_view[pl.ds(1 + 8 * k, 8), pl.ds(8, S), :] = hidden.reshape(8, S, C)
        return carry

    lax.fori_loop(0, 6, forward_first, 0)
    swaps[1].send(edge_strips(padded, 1), choose)
    spread(padded, 0, wide_second, 1, S)
    fill_halo(padded, swaps[1].receive(place), wide_second)

    def forward_second(k, carry):
        pre = jnp.dot(
            taps_of(wide_second, 8 * k),
            weight_second[...].reshape(9 * C, C),
            preferred_element_type=f32,
        )
        below = 0.5 * (1.0 + lax.erf(pre * root_half))
        out_field[pl.ds(8 * k, 8)] = (pre * below).astype(bf16).reshape(8, S, C)
        steep = below + pre * jnp.exp(-0.5 * pre * pre) * inv_root_tau
        cot = cotangent[pl.ds(8 * k, 8)].astype(f32)
        error = (cot * steep.reshape(8, S, C)).astype(bf16).astype(f32)
        delta_view[pl.ds(2 + 8 * k, 8), pl.ds(8, S), :] = error
        return carry

    lax.fori_loop(0, 6, forward_second, 0)
    swaps[2].send(halo_gradients(delta, turned_second), choose)
    weight_gradient(delta, delta_t, wide_second, grad_second)
    second_sum.send_pair()
    spread(delta, 1, wide_delta, 0, 50)
    field_gradient(wide_delta, turned_second, grad)
    add_strips(grad, swaps[2].receive(place))

    def backward_first(k, carry):
        rows = pl.ds(pl.multiple_of(8 * S * k, 8 * S), 8 * S)
        error = (grad[rows, :] * slope[rows, :]).astype(bf16).astype(f32)
        delta_view[pl.ds(2 + 8 * k, 8), pl.ds(8, S), :] = error.reshape(8, S, C)
        return carry

    lax.fori_loop(0, 6, backward_first, 0)
    swaps[3].send(halo_gradients(delta, turned_first), choose)
    second_sum.send_plane()
    weight_gradient(delta, delta_t, wide_first, grad_first)
    first_sum.send_pair()
    spread(delta, 1, wide_delta, 0, 50)
    first_sum.send_plane()
    second_sum.send_column()
    field_gradient(wide_delta, turned_first, grad)
    add_strips(grad, swaps[3].receive(place))
    first_sum.send_column()
    second_sum.send_whole()

    def store(k, carry):
        rows = pl.ds(pl.multiple_of(8 * S * k, 8 * S), 8 * S)
        grad_fields[pl.ds(8 * k, 8)] = grad[rows, :].astype(bf16).reshape(8, S, C)
        return carry

    lax.fori_loop(0, 6, store, 0)
    first_sum.send_whole()
    second_sum.finish(second_out)
    first_sum.finish(first_out)
    for job in swaps + [first_sum, second_sum]:
        job.drain()


def local(fields, weight_first, weight_second, neighbours, cotangent):
    vmem = pl.BlockSpec(memory_space=pltpu.VMEM)
    smem = pl.BlockSpec(memory_space=pltpu.SMEM)
    tile = jax.ShapeDtypeStruct((S, S, C), bf16)
    sums = jax.ShapeDtypeStruct((9, C, C), f32)
    out_field, grad_fields, first, second = pl.pallas_call(
        step_kernel,
        out_shape=(tile, tile, sums, sums),
        in_specs=[vmem, vmem, vmem, smem, vmem],
        out_specs=(vmem, vmem, vmem, vmem),
        scratch_shapes=[
            pltpu.VMEM((50 * PITCH, C), f32),
            pltpu.VMEM((58 * PITCH, C), f32),
            pltpu.VMEM((50, S, 3 * C), bf16),
            pltpu.VMEM((50, S, 3 * C), bf16),
            pltpu.VMEM((50, S, 3 * C), bf16),
            pltpu.VMEM((C, S * S), bf16),
            pltpu.VMEM((S * S, C), f32),
            pltpu.VMEM((S * S, C), f32),
            pltpu.VMEM((C, 9 * C), bf16),
            pltpu.VMEM((C, 9 * C), bf16),
            pltpu.VMEM((4 * SLOT, 4 * SLOT), bf16),
            pltpu.VMEM((4 * SLOT, 4 * SLOT), bf16),
            pltpu.VMEM((4, 4, SLOT, C), bf16),
            pltpu.VMEM((4, 4, SLOT, C), bf16),
            pltpu.SemaphoreType.DMA((4, 2, 4)),
            pltpu.VMEM((9, C, C), f32),
            pltpu.VMEM((9, C, C), f32),
        ]
        + REDUCE_SCRATCH
        + REDUCE_SCRATCH,
        compiler_params=pltpu.CompilerParams(
            collective_id=0, has_side_effects=True, vmem_limit_bytes=60 * 1024 * 1024
        ),
    )(
        fields.reshape(S, S, C),
        weight_first.reshape(9, C, C),
        weight_second.reshape(9, C, C),
        neighbours,
        cotangent.reshape(S, S, C),
    )
    return (
        out_field[None, None],
        grad_fields[None, None],
        first.reshape(3, 3, C, C),
        second.reshape(3, 3, C, C),
    )


def solution(mesh):
    placed = (P("ens", "tile", None, None, None), P(), P(), P(), P("ens", "tile", None, None, None))
    return jax.shard_map(
        local,
        mesh=mesh,
        in_specs=placed,
        out_specs=(
            P("ens", "tile", None, None, None),
            P("ens", "tile", None, None, None),
            P(),
            P(),
        ),
        check_vma=False,
    )
```

```python
import jax
import jax.numpy as jnp
from jax import lax
from jax.experimental import pallas as pl
from jax.experimental.pallas import tpu as pltpu
from jax.sharding import PartitionSpec as P

MESH = pl.DeviceIdType.MESH
root_half = 0.7071067811865476
inv_root_tau = 0.3989422804014327
f32, bf16 = jnp.float32, jnp.bfloat16
S, C = 48, 128
PITCH = 64
SLOT = 64
OFFSETS = (1, -1, 16, -16)


TAPS = 5


class Place:
    def __init__(self):
        ens = lax.axis_index("ens")
        tile = lax.axis_index("tile")
        self.tile = tile
        self.core = tile % 2
        self.z = ens * 4 + (tile // 2) % 4
        self.q = tile // 8

    def device(self, q, z, core):
        return {"ens": z // 4, "tile": q * 8 + (z % 4) * 2 + core}


def greet(me):
    barrier = pltpu.get_barrier_semaphore()

    def signal(target):
        pl.semaphore_signal(barrier, inc=1, device_id=target, device_id_type=MESH)

    def plane(r, carry):
        signal(me.device((me.q + r) % 16, me.z, me.core))
        signal(me.device((me.q + r) % 16, me.z, 1 - me.core))
        return carry

    signal(me.device(me.q, me.z, 1 - me.core))
    lax.fori_loop(1, 16, plane, 0)

    def column(r, carry):
        signal(me.device(me.q, (me.z + r) % 8, me.core))
        return carry

    lax.fori_loop(1, 8, column, 0)
    for step in (1, -1):
        signal({"tile": (me.tile + step) % 128})
    return barrier


class Reduce:
    def __init__(self, me, grad, pair_out, pair_in, part, plane_in, column_in, whole, sems):
        self.me, self.grad = me, grad
        self.pair_out, self.pair_in, self.part = pair_out, pair_in, part
        self.plane_in, self.column_in, self.whole = plane_in, column_in, whole
        self.sems = sems

    def pair_copy(self, part, core):
        slots = pl.ds(2 * (1 - core), 3) if part == 0 else pl.ds(3 * core, 2)
        me = self.me
        return pltpu.make_async_remote_copy(
            src_ref=self.pair_out.at[slots],
            dst_ref=self.pair_in.at[slots],
            send_sem=self.sems.at[0, part],
            recv_sem=self.sems.at[1, part],
            device_id=me.device(me.q, me.z, 1 - me.core),
            device_id_type=MESH,
        )

    def plane_copy(self, target, source):
        return pltpu.make_async_remote_copy(
            src_ref=self.part.at[target],
            dst_ref=self.plane_in.at[source],
            send_sem=self.sems.at[0, 2 + target],
            recv_sem=self.sems.at[1, 2 + source],
            device_id=self.me.device(target, self.me.z, self.me.core),
            device_id_type=MESH,
        )

    def column_copy(self, target, source):
        return pltpu.make_async_remote_copy(
            src_ref=self.column_in.at[source],
            dst_ref=self.column_in.at[source],
            send_sem=self.sems.at[0, 18 + target],
            recv_sem=self.sems.at[1, 18 + source],
            device_id=self.me.device(self.me.q, target, self.me.core),
            device_id_type=MESH,
        )

    def whole_copy(self, target, source):
        core = self.me.core
        return pltpu.make_async_remote_copy(
            src_ref=self.whole.at[core, source],
            dst_ref=self.whole.at[core, source],
            send_sem=self.sems.at[0, 26 + target],
            recv_sem=self.sems.at[1, 26 + source],
            device_id=self.me.device(target, self.me.z, core),
            device_id_type=MESH,
        )

    def relay_copy(self, source, core):
        me = self.me
        return pltpu.make_async_remote_copy(
            src_ref=self.whole.at[core, source],
            dst_ref=self.whole.at[core, source],
            send_sem=self.sems.at[0, 42 + source],
            recv_sem=self.sems.at[1, 42 + source],
            device_id=me.device(me.q, me.z, 1 - me.core),
            device_id_type=MESH,
        )

    def send_pair(self, part):
        core = self.me.core
        for u in range(3 - part):
            if part == 0:
                slot, tap = 2 * (1 - core) + u, 6 * (1 - core) + u
            else:
                slot, tap = 3 * core + u, 4 - core + u
            self.pair_out[slot] = self.grad[tap].astype(bf16)
        self.pair_copy(part, core).start()

    def send_plane(self):
        me = self.me
        for part in range(2):
            self.pair_copy(part, 1 - me.core).wait_recv()

        def band(m, carry):
            rows = pl.ds(pl.multiple_of(16 * m, 16), 16)
            for t in range(TAPS):
                total = self.grad[4 * me.core + t, rows, :] + self.pair_in[t, rows, :].astype(f32)
                self.part[2 * m, t] = total[:8].astype(bf16)
                self.part[2 * m + 1, t] = total[8:].astype(bf16)
            return carry

        lax.fori_loop(0, 8, band, 0)
        self.plane_in[me.q] = self.part[me.q]

        def send(r, carry):
            self.plane_copy((me.q + r) % 16, me.q).start()
            return carry

        lax.fori_loop(1, 16, send, 0)

    def send_column(self):
        me = self.me

        def wait(r, carry):
            self.plane_copy((me.q + r) % 16, (me.q + r) % 16).wait_recv()
            return carry

        lax.fori_loop(1, 16, wait, 0)
        for t in range(TAPS):
            total = self.plane_in[0, t].astype(f32)
            for k in range(1, 16):
                total = total + self.plane_in[k, t].astype(f32)
            self.column_in[me.z, t] = total.astype(bf16)

        def send(r, carry):
            self.column_copy((me.z + r) % 8, me.z).start()
            return carry

        lax.fori_loop(1, 8, send, 0)

    def send_whole(self):
        me = self.me

        def wait(r, carry):
            self.column_copy((me.z + r) % 8, (me.z + r) % 8).wait_recv()
            return carry

        lax.fori_loop(1, 8, wait, 0)
        for t in range(TAPS):
            total = self.column_in[0, t].astype(f32)
            for k in range(1, 8):
                total = total + self.column_in[k, t].astype(f32)
            self.whole[me.core, me.q, t] = total.astype(bf16)

        def send(r, carry):
            self.whole_copy((me.q + r) % 16, me.q).start()
            return carry

        lax.fori_loop(1, 16, send, 0)
        self.relay_copy(me.q, me.core).start()

    def relay(self):
        me = self.me

        def forward(r, carry):
            source = (me.q + r) % 16
            self.whole_copy(source, source).wait_recv()
            self.relay_copy(source, me.core).start()
            return carry

        lax.fori_loop(1, 16, forward, 0)

    def finish(self, out):
        me = self.me

        def wait(r, carry):
            self.relay_copy(r, 1 - me.core).wait_recv()
            return carry

        lax.fori_loop(0, 16, wait, 0)
        for tap in range(9):
            core = 0 if tap < TAPS else 1
            for k in range(16):
                out[tap, 8 * k : 8 * k + 8, :] = self.whole[core, k, tap - 4 * core].astype(
                    f32
                )

    def drain(self):
        me = self.me
        for part in range(2):
            self.pair_copy(part, me.core).wait_send()

        def plane(r, carry):
            target = (me.q + r) % 16
            self.plane_copy(target, me.q).wait_send()
            self.whole_copy(target, me.q).wait_send()
            self.relay_copy(target, me.core).wait_send()
            return carry

        lax.fori_loop(1, 16, plane, 0)
        self.relay_copy(me.q, me.core).wait_send()

        def column(r, carry):
            self.column_copy((me.z + r) % 8, me.z).wait_send()
            return carry

        lax.fori_loop(1, 8, column, 0)


REDUCE_SCRATCH = [
    pltpu.VMEM((TAPS, 128, 128), bf16),
    pltpu.VMEM((TAPS, 128, 128), bf16),
    pltpu.VMEM((16, TAPS, 8, 128), bf16),
    pltpu.VMEM((16, TAPS, 8, 128), bf16),
    pltpu.VMEM((8, TAPS, 8, 128), bf16),
    pltpu.VMEM((2, 16, TAPS, 8, 128), bf16),
    pltpu.SemaphoreType.DMA((2, 58)),
]


class Swap:
    def __init__(self, me, outgoing, incoming, sems):
        self.me, self.outgoing, self.incoming, self.sems = me, outgoing, incoming, sems

    def copy(self, d):
        return pltpu.make_async_remote_copy(
            src_ref=self.outgoing.at[d, pl.ds(0, S)],
            dst_ref=self.incoming.at[d ^ 1, pl.ds(0, S)],
            send_sem=self.sems.at[0, d],
            recv_sem=self.sems.at[1, d ^ 1],
            device_id={"tile": (self.me.tile + OFFSETS[d]) % 128},
            device_id_type=MESH,
        )

    def send(self, strips, choose):
        routed = jnp.dot(choose[...], strips, preferred_element_type=f32).astype(bf16)
        for d in range(4):
            self.outgoing[d] = routed[SLOT * d : SLOT * d + SLOT]
        for d in range(4):
            self.copy(d).start()

    def receive(self, place):
        for d in range(4):
            self.copy(d).wait_recv()
        return jnp.dot(
            place[...], self.incoming[...].reshape(4 * SLOT, C), preferred_element_type=f32
        )

    def drain(self):
        for d in range(4):
            self.copy(d).wait_send()


def routing(me, neighbours, choose, place):
    sides = []
    for offset in OFFSETS:
        target = (me.tile + offset) % 128
        side = jnp.int32(0)
        for s in range(1, 4):
            side = side + jnp.where(neighbours[s, me.tile] == target, s, 0)
        sides.append(side)
    row = lax.broadcasted_iota(jnp.int32, (256, 256), 0)
    col = lax.broadcasted_iota(jnp.int32, (256, 256), 1)
    i, j = row % SLOT, col % SLOT
    inside = (i < S) & (j < S)
    same, flip = inside & (i == j), inside & (i + j == S - 1)

    def side_of(direction):
        out = jnp.full((256, 256), sides[0], jnp.int32)
        for d in range(1, 4):
            out = jnp.where(direction == d, sides[d], out)
        return out

    side = col // SLOT
    hit = (side_of(row // SLOT) == side) & (((side < 2) & same) | ((side >= 2) & flip))
    choose[...] = jnp.where(hit, 1.0, 0.0).astype(bf16)
    side = row // SLOT
    hit = (side_of(col // SLOT) == side) & (((side < 2) & flip) | ((side >= 2) & same))
    place[...] = jnp.where(hit, 1.0, 0.0).astype(bf16)


def pack_strips(strips):
    fill = jnp.zeros((SLOT - S, C), f32)
    return jnp.concatenate(
        [part for strip in strips for part in (strip, fill)], axis=0
    ).astype(bf16)


def border(base, pitch, left):
    start = base * pitch + left
    return (
        pl.ds(start, S),
        pl.ds(start + S - 1, S, stride=pitch),
        pl.ds(start + (S - 1) * pitch, S),
        pl.ds(start, S, stride=pitch),
    )


FLAT = border(0, S, 0)
PADDED = border(1, PITCH, 8)
WIDER = border(2, PITCH, 8)


def spread(padded, base, wide, first, count):
    view = padded.reshape(padded.shape[0] // PITCH, PITCH, C)

    def body(k, carry):
        r = first + k
        for b in range(3):
            wide[r, :, C * b : C * b + C] = view[r + base, pl.ds(7 + b, S), :].astype(bf16)
        return carry

    lax.fori_loop(0, count, body, 0, unroll=4)


def write_ring(padded, halo):
    top, right, bottom, left = (halo[SLOT * s : SLOT * s + S] for s in range(4))
    padded[pl.ds(PITCH + 7, S, stride=PITCH), :] = left
    padded[pl.ds(PITCH + 56, S, stride=PITCH), :] = right
    padded[pl.ds(8, S), :] = top
    padded[pl.ds(PITCH * 49 + 8, S), :] = bottom

    def corner(row, col, one, two):
        padded[pl.ds(PITCH * row + col, 1), :] = (0.5 * (one + two)).astype(bf16).astype(f32)

    corner(0, 7, top[:1], left[:1])
    corner(0, 56, top[S - 1 :], right[:1])
    corner(49, 7, left[S - 1 :], bottom[:1])
    corner(49, 56, bottom[S - 1 :], right[S - 1 :])


def add_halo_terms(padded, weight, pre):
    index = lax.broadcasted_iota(jnp.int32, (S, C), 0)

    def along_row(r):
        return [padded[pl.ds(PITCH * r + 7 + t, S), :] for t in range(3)]

    def along_column(col):
        lines = [padded[pl.ds(PITCH * t + col, S, stride=PITCH), :] for t in range(3)]
        lines[0] = jnp.where(index == 0, 0.0, lines[0])
        lines[2] = jnp.where(index == S - 1, 0.0, lines[2])
        return lines

    sides = (
        (along_row(0), (0, 1, 2)),
        (along_column(56), (2, 5, 8)),
        (along_row(49), (6, 7, 8)),
        (along_column(7), (0, 3, 6)),
    )
    terms = [
        jnp.dot(
            jnp.concatenate(lines, axis=1).astype(bf16),
            jnp.concatenate([weight[t] for t in taps], axis=0),
            preferred_element_type=f32,
        )
        for lines, taps in sides
    ]
    for where, term in zip(FLAT, terms):
        pre[where, :] += term


def spread_halo(padded, wide):
    view = padded.reshape(50, PITCH, C)
    for r in (0, 49):
        for b in range(3):
            wide[r, :, C * b : C * b + C] = view[r, pl.ds(7 + b, S), :].astype(bf16)

    def body(k, carry):
        r = 1 + k
        wide[r, :16, :C] = view[r, pl.ds(7, 16), :].astype(bf16)
        wide[r, 32:, 2 * C :] = view[r, pl.ds(41, 16), :].astype(bf16)
        return carry

    lax.fori_loop(0, S, body, 0, unroll=4)


def clear_ring(padded, rows, first):
    view = padded.reshape(padded.shape[0] // PITCH, PITCH, C)
    for r in rows:
        view[r] = jnp.zeros((PITCH, C), f32)
    view[first : first + S, :8, :] = jnp.zeros((S, 8, C), f32)
    view[first : first + S, 56:, :] = jnp.zeros((S, 8, C), f32)


def gelu(pre):
    below = 0.5 * (1.0 + lax.erf(pre * root_half))
    return pre * below, below + pre * jnp.exp(-0.5 * pre * pre) * inv_root_tau


def rounded(value):
    return value.astype(bf16).astype(f32)


def block(k):
    return pl.ds(pl.multiple_of(8 * S * k, 8 * S), 8 * S)


def taps_of(wide, start):
    return jnp.concatenate(
        [wide[pl.ds(start + a, 8)].reshape(8 * S, 3 * C) for a in range(3)], axis=1
    )


def dot_rows(rows, weight):
    return lax.dot_general(rows, weight, (((1,), (1,)), ((), ())), preferred_element_type=f32)


def halo_gradients(delta, turned):
    index = lax.broadcasted_iota(jnp.int32, (S, C), 0)

    def along_row(i):
        return [delta[pl.ds(PITCH * (i + 2) + 6 + t, 56), :] for t in range(3)]

    def along_column(j):
        return [delta[pl.ds(PITCH * t + 8 + j, 56, stride=PITCH), :] for t in range(3)]

    def tap(a, b):
        return turned[:, C * (3 * a + b) : C * (3 * a + b) + C]

    sides = (
        (along_row(0), [tap(2, t) for t in range(3)]),
        (along_column(S - 1), [tap(t, 0) for t in range(3)]),
        (along_row(S - 1), [tap(0, t) for t in range(3)]),
        (along_column(0), [tap(t, 2) for t in range(3)]),
    )
    parts = []
    for lines, blocks in sides:
        full = dot_rows(
            jnp.concatenate(lines, axis=1).astype(bf16), jnp.concatenate(blocks, axis=1)
        )
        strip = full[1 : S + 1]
        strip = strip + jnp.where(index == 0, 0.5 * full[:1], 0.0)
        strip = strip + jnp.where(index == S - 1, 0.5 * full[S + 1 : S + 2], 0.0)
        parts.append(strip)
    return pack_strips(parts)


def turn(weight, turned):
    for k in range(9):
        turned[:, C * k : C * k + C] = weight[8 - k]


def weight_gradient(me, delta, delta_t, wide, total):
    view = delta.reshape(delta.shape[0] // PITCH, PITCH, C)
    for k in range(6):
        rows = view[pl.ds(2 + 8 * k, 8), pl.ds(8, S), :].reshape(8 * S, C)
        delta_t[:, 8 * S * k : 8 * S * (k + 1)] = rows.T.astype(bf16)

    def tap_row(i):
        a = (1 - me.core) * (2 - i) + me.core * i
        flat = wide[pl.ds(a, S)].reshape(S * S, 3 * C)
        product = jnp.dot(delta_t[...], flat, preferred_element_type=f32)
        for b in range(3):
            total.grad[3 * a + b] = product[:, C * b : C * b + C].T

    for i in range(3):
        tap_row(i)
        if i < 2:
            total.send_pair(i)


def field_gradient(wide, turned, grad):
    def body(k, carry):
        grad[block(k), :] = dot_rows(taps_of(wide, 8 * k), turned[...])
        return carry

    lax.fori_loop(0, 6, body, 0)


def add_strips(grad, strips):
    for s in range(4):
        grad[FLAT[s], :] += strips[SLOT * s : SLOT * s + S]


def step_kernel(
    fields_hbm, weight_first_hbm, weight_second_hbm, neighbours, cotangent_hbm,
    out_field, grad_fields, first_out, second_out,
    fields, weight_first, weight_second, cotangent, load_sems,
    padded_first, padded_second, delta, wide_first, wide_second, wide_delta, delta_t,
    pre, slope, value, grad,
    turned_first, turned_second, choose, place, outgoing, incoming, swap_sems,
    grad_first, grad_second, *reduce_scratch,
):
    loads = [
        pltpu.make_async_copy(source, target, load_sems.at[n])
        for n, (source, target) in enumerate(
            (
                (fields_hbm, fields),
                (weight_first_hbm, weight_first),
                (weight_second_hbm, weight_second),
                (cotangent_hbm, cotangent),
            )
        )
    ]
    for load in loads:
        load.start()
    me = Place()
    barrier = greet(me)
    half = len(REDUCE_SCRATCH)
    second_sum = Reduce(me, grad_second, *reduce_scratch[:half])
    first_sum = Reduce(me, grad_first, *reduce_scratch[half:])
    swaps = [Swap(me, outgoing.at[e], incoming.at[e], swap_sems.at[e]) for e in range(4)]

    routing(me, neighbours, choose, place)
    incoming[:, :, S:, :] = jnp.zeros((4, 4, SLOT - S, C), bf16)
    clear_ring(padded_first, (0, 49), 1)
    clear_ring(padded_second, (0, 49), 1)
    clear_ring(delta, (0, 1, 50, 51, 52, 53, 54, 55, 56, 57), 2)
    first_view = padded_first.reshape(50, PITCH, C)
    second_view = padded_second.reshape(50, PITCH, C)
    delta_view = delta.reshape(58, PITCH, C)
    loads[0].wait()

    def load_fields(k, carry):
        first_view[pl.ds(1 + 8 * k, 8), pl.ds(8, S), :] = fields[pl.ds(8 * k, 8)].astype(f32)
        return carry

    lax.fori_loop(0, 6, load_fields, 0)
    strips = pack_strips([padded_first[where, :] for where in PADDED])
    pl.semaphore_wait(barrier, 40)
    swaps[0].send(strips, choose)

    spread(padded_first, 0, wide_first, 0, 50)
    loads[1].wait()

    def forward_first(k, carry):
        now = jnp.dot(
            taps_of(wide_first, 8 * k),
            weight_first[...].reshape(9 * C, C),
            preferred_element_type=f32,
        )
        pre[block(k), :] = now
        hidden, steep = gelu(now)
        slope[block(k), :] = steep
        second_view[pl.ds(1 + 8 * k, 8), pl.ds(8, S), :] = rounded(hidden).reshape(8, S, C)
        return carry

    lax.fori_loop(0, 6, forward_first, 0)
    write_ring(padded_first, swaps[0].receive(place))
    add_halo_terms(padded_first, weight_first, pre)
    strips = []
    for s in range(4):
        hidden, steep = gelu(pre[FLAT[s], :])
        hidden = rounded(hidden)
        slope[FLAT[s], :] = steep
        padded_second[PADDED[s], :] = hidden
        strips.append(hidden)
    swaps[1].send(pack_strips(strips), choose)

    spread(padded_second, 0, wide_second, 0, 50)
    loads[2].wait()
    loads[3].wait()

    def forward_second(k, carry):
        now = jnp.dot(
            taps_of(wide_second, 8 * k),
            weight_second[...].reshape(9 * C, C),
            preferred_element_type=f32,
        )
        pre[block(k), :] = now
        out, steep = gelu(now)
        value[block(k), :] = out
        cot = cotangent[pl.ds(8 * k, 8)].astype(f32)
        grad[block(k), :] = cot.reshape(8 * S, C)
        error = cot * steep.reshape(8, S, C)
        delta_view[pl.ds(2 + 8 * k, 8), pl.ds(8, S), :] = rounded(error)
        return carry

    lax.fori_loop(0, 6, forward_second, 0)
    turn(weight_second, turned_second)
    turn(weight_first, turned_first)
    spread_halo(padded_first, wide_first)
    write_ring(padded_second, swaps[1].receive(place))
    add_halo_terms(padded_second, weight_second, pre)
    for s in range(4):
        out, steep = gelu(pre[FLAT[s], :])
        value[FLAT[s], :] = out
        delta[WIDER[s], :] = rounded(grad[FLAT[s], :] * steep)
    swaps[2].send(halo_gradients(delta, turned_second), choose)

    spread_halo(padded_second, wide_second)
    weight_gradient(me, delta, delta_t, wide_second, second_sum)
    spread(delta, 1, wide_delta, 0, 50)
    second_sum.send_plane()
    field_gradient(wide_delta, turned_second, grad)
    add_strips(grad, swaps[2].receive(place))

    def backward_first(k, carry):
        error = rounded(grad[block(k), :] * slope[block(k), :])
        delta_view[pl.ds(2 + 8 * k, 8), pl.ds(8, S), :] = error.reshape(8, S, C)
        return carry

    lax.fori_loop(0, 6, backward_first, 0)
    weight_gradient(me, delta, delta_t, wide_first, first_sum)
    swaps[3].send(halo_gradients(delta, turned_first), choose)
    first_sum.send_plane()
    second_sum.send_column()
    spread(delta, 1, wide_delta, 0, 50)
    field_gradient(wide_delta, turned_first, grad)
    add_strips(grad, swaps[3].receive(place))
    first_sum.send_column()
    second_sum.send_whole()

    def store(k, carry):
        grad_fields[pl.ds(8 * k, 8)] = grad[block(k), :].astype(bf16).reshape(8, S, C)
        out_field[pl.ds(8 * k, 8)] = value[block(k), :].astype(bf16).reshape(8, S, C)
        return carry

    lax.fori_loop(0, 6, store, 0)
    first_sum.send_whole()
    second_sum.relay()
    second_sum.finish(second_out)
    first_sum.relay()
    first_sum.finish(first_out)
    for job in swaps + [first_sum, second_sum]:
        job.drain()


def store_kernel(*refs):
    copies = [
        pltpu.make_async_copy(refs[n], refs[4 + n], refs[8].at[n]) for n in range(4)
    ]
    for copy in copies:
        copy.start()
    for copy in copies:
        copy.wait()


def local(fields, weight_first, weight_second, neighbours, cotangent):
    vmem = pl.BlockSpec(memory_space=pltpu.VMEM)
    smem = pl.BlockSpec(memory_space=pltpu.SMEM)
    hbm = pl.BlockSpec(memory_space=pltpu.HBM)
    tile = (S, S, C)
    sums = (9, C, C)
    results = pl.pallas_call(
        step_kernel,
        out_shape=(
            pltpu.VMEM(tile, bf16),
            pltpu.VMEM(tile, bf16),
            pltpu.VMEM(sums, f32),
            pltpu.VMEM(sums, f32),
        ),
        in_specs=[hbm, hbm, hbm, smem, hbm],
        out_specs=(vmem, vmem, vmem, vmem),
        scratch_shapes=[
            pltpu.VMEM(tile, bf16),
            pltpu.VMEM(sums, bf16),
            pltpu.VMEM(sums, bf16),
            pltpu.VMEM(tile, bf16),
            pltpu.SemaphoreType.DMA((4,)),
            pltpu.VMEM((50 * PITCH, C), f32),
            pltpu.VMEM((50 * PITCH, C), f32),
            pltpu.VMEM((58 * PITCH, C), f32),
            pltpu.VMEM((50, S, 3 * C), bf16),
            pltpu.VMEM((50, S, 3 * C), bf16),
            pltpu.VMEM((50, S, 3 * C), bf16),
            pltpu.VMEM((C, S * S), bf16),
            pltpu.VMEM((S * S, C), f32),
            pltpu.VMEM((S * S, C), f32),
            pltpu.VMEM((S * S, C), f32),
            pltpu.VMEM((S * S, C), f32),
            pltpu.VMEM((C, 9 * C), bf16),
            pltpu.VMEM((C, 9 * C), bf16),
            pltpu.VMEM((4 * SLOT, 4 * SLOT), bf16),
            pltpu.VMEM((4 * SLOT, 4 * SLOT), bf16),
            pltpu.VMEM((4, 4, SLOT, C), bf16),
            pltpu.VMEM((4, 4, SLOT, C), bf16),
            pltpu.SemaphoreType.DMA((4, 2, 4)),
            pltpu.VMEM(sums, f32),
            pltpu.VMEM(sums, f32),
        ]
        + REDUCE_SCRATCH
        + REDUCE_SCRATCH,
        compiler_params=pltpu.CompilerParams(
            collective_id=0, has_side_effects=True, vmem_limit_bytes=64_500_000
        ),
    )(
        fields.reshape(tile),
        weight_first.reshape(sums),
        weight_second.reshape(sums),
        neighbours.T,
        cotangent.reshape(tile),
    )
    out_field, grad_fields, first, second = pl.pallas_call(
        store_kernel,
        out_shape=(
            jax.ShapeDtypeStruct(tile, bf16),
            jax.ShapeDtypeStruct(tile, bf16),
            jax.ShapeDtypeStruct(sums, f32),
            jax.ShapeDtypeStruct(sums, f32),
        ),
        in_specs=[vmem, vmem, vmem, vmem],
        out_specs=(hbm, hbm, hbm, hbm),
        scratch_shapes=[pltpu.SemaphoreType.DMA((4,))],
        compiler_params=pltpu.CompilerParams(vmem_limit_bytes=1024 * 1024),
    )(*results)
    return (
        out_field[None, None],
        grad_fields[None, None],
        first.reshape(3, 3, C, C),
        second.reshape(3, 3, C, C),
    )


def solution(mesh):
    placed = (P("ens", "tile", None, None, None), P(), P(), P(), P("ens", "tile", None, None, None))
    return jax.shard_map(
        local,
        mesh=mesh,
        in_specs=placed,
        out_specs=(
            P("ens", "tile", None, None, None),
            P("ens", "tile", None, None, None),
            P(),
            P(),
        ),
        check_vma=False,
    )
```

```python
import jax
import jax.numpy as jnp
from jax import lax
from jax.experimental import pallas as pl
from jax.experimental.pallas import tpu as pltpu
from jax.sharding import PartitionSpec as P

MESH = pl.DeviceIdType.MESH
root_half = 0.7071067811865476
inv_root_tau = 0.3989422804014327
f32, bf16 = jnp.float32, jnp.bfloat16
S, C = 48, 128
PITCH = 64
SLOT = 64
OFFSETS = (1, -1, 16, -16)


TAPS = 5
FAR_FIRST = sorted(
    ((dx, dy) for dx in range(4) for dy in range(4) if dx or dy),
    key=lambda d: -(min(d[0], 4 - d[0]) + min(d[1], 4 - d[1])),
)


class Place:
    def __init__(self):
        ens = lax.axis_index("ens")
        tile = lax.axis_index("tile")
        self.tile = tile
        self.core = tile % 2
        self.z = ens * 4 + (tile // 2) % 4
        self.q = tile // 8

    def plane(self):
        x, y = self.q // 4, self.q % 4
        return [((x + dx) % 4) * 4 + (y + dy) % 4 for dx, dy in FAR_FIRST]

    def device(self, q, z, core):
        return {"ens": z // 4, "tile": q * 8 + (z % 4) * 2 + core}


def greet(me):
    barrier = pltpu.get_barrier_semaphore()

    def signal(target):
        pl.semaphore_signal(barrier, inc=1, device_id=target, device_id_type=MESH)

    def plane(r, carry):
        signal(me.device((me.q + r) % 16, me.z, me.core))
        signal(me.device((me.q + r) % 16, me.z, 1 - me.core))
        return carry

    signal(me.device(me.q, me.z, 1 - me.core))
    lax.fori_loop(1, 16, plane, 0)

    def column(r, carry):
        signal(me.device(me.q, (me.z + r) % 8, me.core))
        return carry

    lax.fori_loop(1, 8, column, 0)
    for step in (1, -1):
        signal({"tile": (me.tile + step) % 128})
    return barrier


class Reduce:
    def __init__(self, me, grad, pair_out, pair_in, part, plane_in, column_in, whole, sems):
        self.me, self.grad = me, grad
        self.pair_out, self.pair_in, self.part = pair_out, pair_in, part
        self.plane_in, self.column_in, self.whole = plane_in, column_in, whole
        self.sems = sems

    def pair_copy(self, part, core):
        slots = pl.ds(2 * (1 - core), 3) if part == 0 else pl.ds(3 * core, 2)
        me = self.me
        return pltpu.make_async_remote_copy(
            src_ref=self.pair_out.at[slots],
            dst_ref=self.pair_in.at[slots],
            send_sem=self.sems.at[0, part],
            recv_sem=self.sems.at[1, part],
            device_id=me.device(me.q, me.z, 1 - me.core),
            device_id_type=MESH,
        )

    def plane_copy(self, target, source):
        return pltpu.make_async_remote_copy(
            src_ref=self.part.at[target],
            dst_ref=self.plane_in.at[source],
            send_sem=self.sems.at[0, 2],
            recv_sem=self.sems.at[1, 2],
            device_id=self.me.device(target, self.me.z, self.me.core),
            device_id_type=MESH,
        )

    def column_copy(self, target, source):
        return pltpu.make_async_remote_copy(
            src_ref=self.column_in.at[source],
            dst_ref=self.column_in.at[source],
            send_sem=self.sems.at[0, 3],
            recv_sem=self.sems.at[1, 3],
            device_id=self.me.device(self.me.q, target, self.me.core),
            device_id_type=MESH,
        )

    def whole_copy(self, target, source):
        core = self.me.core
        return pltpu.make_async_remote_copy(
            src_ref=self.whole.at[core, source],
            dst_ref=self.whole.at[core, source],
            send_sem=self.sems.at[0, 4],
            recv_sem=self.sems.at[1, 4],
            device_id=self.me.device(target, self.me.z, core),
            device_id_type=MESH,
        )

    def relay_copy(self, core):
        me = self.me
        return pltpu.make_async_remote_copy(
            src_ref=self.whole.at[core],
            dst_ref=self.whole.at[core],
            send_sem=self.sems.at[0, 5],
            recv_sem=self.sems.at[1, 5],
            device_id=me.device(me.q, me.z, 1 - me.core),
            device_id_type=MESH,
        )

    def stage(self, source, target, index):
        me = self.me
        return pltpu.make_async_remote_copy(
            src_ref=source,
            dst_ref=target,
            send_sem=self.sems.at[0, index],
            recv_sem=self.sems.at[1, index],
            device_id=me.device(me.q, me.z, 1 - me.core),
            device_id_type=MESH,
        )

    def plane_stage(self):
        return self.stage(self.part.at[pl.ds(0, 15)], self.plane_in.at[pl.ds(0, 15)], 2)

    def column_stage(self):
        return self.stage(self.column_in.at[pl.ds(0, 7)], self.column_in.at[pl.ds(0, 7)], 3)

    def whole_stage(self):
        blocks = self.whole.at[self.me.core, pl.ds(0, 15)]
        return self.stage(blocks, blocks, 4)

    def send_pair(self, part):
        core = self.me.core
        for u in range(3 - part):
            if part == 0:
                slot, tap = 2 * (1 - core) + u, 6 * (1 - core) + u
            else:
                slot, tap = 3 * core + u, 4 - core + u
            self.pair_out[slot] = self.grad[tap].astype(bf16)
        self.pair_copy(part, core).start()

    def send_plane(self):
        me = self.me
        for part in range(2):
            self.pair_copy(part, 1 - me.core).wait_recv()

        def band(m, carry):
            rows = pl.ds(pl.multiple_of(16 * m, 16), 16)
            for t in range(TAPS):
                total = self.grad[4 * me.core + t, rows, :] + self.pair_in[t, rows, :].astype(f32)
                self.part[2 * m, t] = total[:8].astype(bf16)
                self.part[2 * m + 1, t] = total[8:].astype(bf16)
            return carry

        lax.fori_loop(0, 8, band, 0)
        self.plane_in[me.q] = self.part[me.q]

        for target in me.plane():
            self.plane_copy(target, me.q).start()

    def send_column(self):
        me = self.me
        self.plane_stage().wait_recv()
        for t in range(TAPS):
            total = self.plane_in[0, t].astype(f32)
            for k in range(1, 16):
                total = total + self.plane_in[k, t].astype(f32)
            self.column_in[me.z, t] = total.astype(bf16)

        for r in (4, 3, 5, 2, 6, 1, 7):
            self.column_copy((me.z + r) % 8, me.z).start()

    def send_whole(self):
        me = self.me
        self.column_stage().wait_recv()
        for t in range(TAPS):
            total = self.column_in[0, t].astype(f32)
            for k in range(1, 8):
                total = total + self.column_in[k, t].astype(f32)
            self.whole[me.core, me.q, t] = total.astype(bf16)

        for target in me.plane():
            self.whole_copy(target, me.q).start()

    def relay(self):
        self.whole_stage().wait_recv()
        self.relay_copy(self.me.core).start()

    def finish(self, out, core):
        def body(k, carry):
            rows = pl.ds(pl.multiple_of(8 * k, 8), 8)
            for u in range(4):
                out[5 * core + u, rows, :] = self.whole[core, k, core + u].astype(f32)
            return carry

        lax.fori_loop(0, 16, body, 0, unroll=4)

    def finish_own(self, out):
        self.finish(out, self.me.core)

    def finish_other(self, out):
        me = self.me

        self.relay_copy(1 - me.core).wait_recv()
        self.finish(out, 1 - me.core)
        for k in range(16):
            out[4, 8 * k : 8 * k + 8, :] = self.whole[0, k, 4].astype(f32)

    def drain(self):
        me = self.me
        for part in range(2):
            self.pair_copy(part, me.core).wait_send()
        self.plane_stage().wait_send()
        self.column_stage().wait_send()
        self.whole_stage().wait_send()
        self.relay_copy(me.core).wait_send()


REDUCE_SCRATCH = [
    pltpu.VMEM((TAPS, 128, 128), bf16),
    pltpu.VMEM((TAPS, 128, 128), bf16),
    pltpu.VMEM((16, TAPS, 8, 128), bf16),
    pltpu.VMEM((16, TAPS, 8, 128), bf16),
    pltpu.VMEM((8, TAPS, 8, 128), bf16),
    pltpu.VMEM((2, 16, TAPS, 8, 128), bf16),
    pltpu.SemaphoreType.DMA((2, 6)),
]


class Swap:
    def __init__(self, me, outgoing, incoming, sems):
        self.me, self.outgoing, self.incoming, self.sems = me, outgoing, incoming, sems

    def copy(self, d):
        return pltpu.make_async_remote_copy(
            src_ref=self.outgoing.at[d, pl.ds(0, S)],
            dst_ref=self.incoming.at[d ^ 1, pl.ds(0, S)],
            send_sem=self.sems.at[0],
            recv_sem=self.sems.at[1],
            device_id={"tile": (self.me.tile + OFFSETS[d]) % 128},
            device_id_type=MESH,
        )

    def send(self, strips, choose):
        routed = jnp.dot(choose[...], strips, preferred_element_type=f32).astype(bf16)
        for d in range(4):
            self.outgoing[d] = routed[SLOT * d : SLOT * d + SLOT]
        for d in range(4):
            self.copy(d).start()

    def receive(self, place):
        self.everything().wait_recv()
        return jnp.dot(
            place[...], self.incoming[...].reshape(4 * SLOT, C), preferred_element_type=f32
        )

    def everything(self):
        return pltpu.make_async_remote_copy(
            src_ref=self.outgoing.at[:, pl.ds(0, S)],
            dst_ref=self.incoming.at[:, pl.ds(0, S)],
            send_sem=self.sems.at[0],
            recv_sem=self.sems.at[1],
            device_id={"tile": (self.me.tile + 1) % 128},
            device_id_type=MESH,
        )

    def drain(self):
        self.everything().wait_send()


def routing(me, neighbours, choose, place):
    sides = []
    for offset in OFFSETS:
        target = (me.tile + offset) % 128
        side = jnp.int32(0)
        for s in range(1, 4):
            side = side + jnp.where(neighbours[s, me.tile] == target, s, 0)
        sides.append(side)
    row = lax.broadcasted_iota(jnp.int32, (256, 256), 0)
    col = lax.broadcasted_iota(jnp.int32, (256, 256), 1)
    i, j = row % SLOT, col % SLOT
    inside = (i < S) & (j < S)
    same, flip = inside & (i == j), inside & (i + j == S - 1)

    def side_of(direction):
        out = jnp.full((256, 256), sides[0], jnp.int32)
        for d in range(1, 4):
            out = jnp.where(direction == d, sides[d], out)
        return out

    side = col // SLOT
    hit = (side_of(row // SLOT) == side) & (((side < 2) & same) | ((side >= 2) & flip))
    choose[...] = jnp.where(hit, 1.0, 0.0).astype(bf16)
    side = row // SLOT
    hit = (side_of(col // SLOT) == side) & (((side < 2) & flip) | ((side >= 2) & same))
    place[...] = jnp.where(hit, 1.0, 0.0).astype(bf16)


def pack_strips(strips):
    fill = jnp.zeros((SLOT - S, C), f32)
    return jnp.concatenate(
        [part for strip in strips for part in (strip, fill)], axis=0
    ).astype(bf16)


def border(base, pitch, left):
    start = base * pitch + left
    return (
        pl.ds(start, S),
        pl.ds(start + S - 1, S, stride=pitch),
        pl.ds(start + (S - 1) * pitch, S),
        pl.ds(start, S, stride=pitch),
    )


FLAT = border(0, S, 0)
PADDED = border(1, PITCH, 8)
WIDER = border(2, PITCH, 8)


def spread(padded, base, wide, first, count):
    view = padded.reshape(padded.shape[0] // PITCH, PITCH, C)

    def body(k, carry):
        r = first + k
        for b in range(3):
            wide[r, :, C * b : C * b + C] = view[r + base, pl.ds(7 + b, S), :].astype(bf16)
        return carry

    lax.fori_loop(0, count, body, 0, unroll=4)


def write_ring(padded, halo):
    top, right, bottom, left = (halo[SLOT * s : SLOT * s + S] for s in range(4))
    padded[pl.ds(PITCH + 7, S, stride=PITCH), :] = left
    padded[pl.ds(PITCH + 56, S, stride=PITCH), :] = right
    padded[pl.ds(8, S), :] = top
    padded[pl.ds(PITCH * 49 + 8, S), :] = bottom

    def corner(row, col, one, two):
        padded[pl.ds(PITCH * row + col, 1), :] = (0.5 * (one + two)).astype(bf16).astype(f32)

    corner(0, 7, top[:1], left[:1])
    corner(0, 56, top[S - 1 :], right[:1])
    corner(49, 7, left[S - 1 :], bottom[:1])
    corner(49, 56, bottom[S - 1 :], right[S - 1 :])


def add_halo_terms(padded, weight, pre):
    index = lax.broadcasted_iota(jnp.int32, (S, C), 0)

    def along_row(r):
        return [padded[pl.ds(PITCH * r + 7 + t, S), :] for t in range(3)]

    def along_column(col):
        lines = [padded[pl.ds(PITCH * t + col, S, stride=PITCH), :] for t in range(3)]
        lines[0] = jnp.where(index == 0, 0.0, lines[0])
        lines[2] = jnp.where(index == S - 1, 0.0, lines[2])
        return lines

    sides = (
        (along_row(0), (0, 1, 2)),
        (along_column(56), (2, 5, 8)),
        (along_row(49), (6, 7, 8)),
        (along_column(7), (0, 3, 6)),
    )
    terms = [
        jnp.dot(
            jnp.concatenate(lines, axis=1).astype(bf16),
            jnp.concatenate([weight[t] for t in taps], axis=0),
            preferred_element_type=f32,
        )
        for lines, taps in sides
    ]
    for where, term in zip(FLAT, terms):
        pre[where, :] += term


def spread_halo(padded, wide):
    view = padded.reshape(50, PITCH, C)
    for r in (0, 49):
        for b in range(3):
            wide[r, :, C * b : C * b + C] = view[r, pl.ds(7 + b, S), :].astype(bf16)

    def body(k, carry):
        r = 1 + k
        wide[r, :16, :C] = view[r, pl.ds(7, 16), :].astype(bf16)
        wide[r, 32:, 2 * C :] = view[r, pl.ds(41, 16), :].astype(bf16)
        return carry

    lax.fori_loop(0, S, body, 0, unroll=4)


def clear_ring(padded, rows, first):
    view = padded.reshape(padded.shape[0] // PITCH, PITCH, C)
    for r in rows:
        view[r] = jnp.zeros((PITCH, C), f32)
    view[first : first + S, :8, :] = jnp.zeros((S, 8, C), f32)
    view[first : first + S, 56:, :] = jnp.zeros((S, 8, C), f32)


def gelu(pre):
    below = 0.5 * (1.0 + lax.erf(pre * root_half))
    return pre * below, below + pre * jnp.exp(-0.5 * pre * pre) * inv_root_tau


def rounded(value):
    return value.astype(bf16).astype(f32)


def block(k):
    return pl.ds(pl.multiple_of(8 * S * k, 8 * S), 8 * S)


def taps_of(wide, start):
    return jnp.concatenate(
        [wide[pl.ds(start + a, 8)].reshape(8 * S, 3 * C) for a in range(3)], axis=1
    )


def dot_rows(rows, weight):
    return lax.dot_general(rows, weight, (((1,), (1,)), ((), ())), preferred_element_type=f32)


def halo_gradients(delta, turned):
    index = lax.broadcasted_iota(jnp.int32, (S, C), 0)

    def along_row(i):
        return [delta[pl.ds(PITCH * (i + 2) + 6 + t, 56), :] for t in range(3)]

    def along_column(j):
        return [delta[pl.ds(PITCH * t + 8 + j, 56, stride=PITCH), :] for t in range(3)]

    def tap(a, b):
        return turned[:, C * (3 * a + b) : C * (3 * a + b) + C]

    sides = (
        (along_row(0), [tap(2, t) for t in range(3)]),
        (along_column(S - 1), [tap(t, 0) for t in range(3)]),
        (along_row(S - 1), [tap(0, t) for t in range(3)]),
        (along_column(0), [tap(t, 2) for t in range(3)]),
    )
    parts = []
    for lines, blocks in sides:
        full = dot_rows(
            jnp.concatenate(lines, axis=1).astype(bf16), jnp.concatenate(blocks, axis=1)
        )
        strip = full[1 : S + 1]
        strip = strip + jnp.where(index == 0, 0.5 * full[:1], 0.0)
        strip = strip + jnp.where(index == S - 1, 0.5 * full[S + 1 : S + 2], 0.0)
        parts.append(strip)
    return pack_strips(parts)


def turn(weight, turned):
    for k in range(9):
        turned[:, C * k : C * k + C] = weight[8 - k]


def weight_gradient(me, delta, delta_t, wide, total):
    view = delta.reshape(delta.shape[0] // PITCH, PITCH, C)
    for k in range(6):
        rows = view[pl.ds(2 + 8 * k, 8), pl.ds(8, S), :].reshape(8 * S, C)
        delta_t[:, 8 * S * k : 8 * S * (k + 1)] = rows.T.astype(bf16)

    def tap_row(i):
        a = (1 - me.core) * (2 - i) + me.core * i
        flat = wide[pl.ds(a, S)].reshape(S * S, 3 * C)
        product = jnp.dot(delta_t[...], flat, preferred_element_type=f32)
        for b in range(3):
            total.grad[3 * a + b] = product[:, C * b : C * b + C].T

    for i in range(3):
        tap_row(i)
        if i < 2:
            total.send_pair(i)


def field_gradient(wide, turned, grad):
    def body(k, carry):
        grad[block(k), :] = dot_rows(taps_of(wide, 8 * k), turned[...])
        return carry

    lax.fori_loop(0, 6, body, 0)


def add_strips(grad, strips):
    for s in range(4):
        grad[FLAT[s], :] += strips[SLOT * s : SLOT * s + S]


def step_kernel(
    fields_hbm, weight_first_hbm, weight_second_hbm, neighbours, cotangent_hbm,
    out_field, grad_fields, first_out, second_out,
    fields, weight_first, weight_second, cotangent, load_sems,
    padded_first, padded_second, delta, wide_first, wide_second, wide_delta, delta_t,
    pre, slope, value, grad,
    turned_first, turned_second, choose, place, outgoing, incoming, swap_sems,
    grad_first, grad_second, *reduce_scratch,
):
    loads = [
        pltpu.make_async_copy(source, target, load_sems.at[n])
        for n, (source, target) in enumerate(
            (
                (fields_hbm, fields),
                (weight_first_hbm, weight_first),
                (weight_second_hbm, weight_second),
                (cotangent_hbm, cotangent),
            )
        )
    ]
    for load in loads:
        load.start()
    me = Place()
    barrier = greet(me)
    half = len(REDUCE_SCRATCH)
    second_sum = Reduce(me, grad_second, *reduce_scratch[:half])
    first_sum = Reduce(me, grad_first, *reduce_scratch[half:])
    swaps = [Swap(me, outgoing.at[e], incoming.at[e], swap_sems.at[e]) for e in range(4)]

    routing(me, neighbours, choose, place)
    incoming[:, :, S:, :] = jnp.zeros((4, 4, SLOT - S, C), bf16)
    clear_ring(padded_first, (0, 49), 1)
    clear_ring(padded_second, (0, 49), 1)
    clear_ring(delta, (0, 1, 50, 51, 52, 53, 54, 55, 56, 57), 2)
    first_view = padded_first.reshape(50, PITCH, C)
    second_view = padded_second.reshape(50, PITCH, C)
    delta_view = delta.reshape(58, PITCH, C)
    loads[0].wait()

    def load_fields(k, carry):
        first_view[pl.ds(1 + 8 * k, 8), pl.ds(8, S), :] = fields[pl.ds(8 * k, 8)].astype(f32)
        return carry

    lax.fori_loop(0, 6, load_fields, 0)
    strips = pack_strips([padded_first[where, :] for where in PADDED])
    pl.semaphore_wait(barrier, 40)
    swaps[0].send(strips, choose)

    spread(padded_first, 0, wide_first, 0, 50)
    loads[1].wait()

    def forward_first(k, carry):
        now = jnp.dot(
            taps_of(wide_first, 8 * k),
            weight_first[...].reshape(9 * C, C),
            preferred_element_type=f32,
        )
        pre[block(k), :] = now
        hidden, steep = gelu(now)
        slope[block(k), :] = steep
        second_view[pl.ds(1 + 8 * k, 8), pl.ds(8, S), :] = rounded(hidden).reshape(8, S, C)
        return carry

    lax.fori_loop(0, 6, forward_first, 0)
    write_ring(padded_first, swaps[0].receive(place))
    add_halo_terms(padded_first, weight_first, pre)
    strips = []
    for s in range(4):
        hidden, steep = gelu(pre[FLAT[s], :])
        hidden = rounded(hidden)
        slope[FLAT[s], :] = steep
        padded_second[PADDED[s], :] = hidden
        strips.append(hidden)
    swaps[1].send(pack_strips(strips), choose)

    spread(padded_second, 0, wide_second, 0, 50)
    loads[2].wait()
    loads[3].wait()

    def forward_second(k, carry):
        now = jnp.dot(
            taps_of(wide_second, 8 * k),
            weight_second[...].reshape(9 * C, C),
            preferred_element_type=f32,
        )
        pre[block(k), :] = now
        out, steep = gelu(now)
        value[block(k), :] = out
        cot = cotangent[pl.ds(8 * k, 8)].astype(f32)
        grad[block(k), :] = cot.reshape(8 * S, C)
        error = cot * steep.reshape(8, S, C)
        delta_view[pl.ds(2 + 8 * k, 8), pl.ds(8, S), :] = rounded(error)
        return carry

    lax.fori_loop(0, 6, forward_second, 0)
    turn(weight_second, turned_second)
    turn(weight_first, turned_first)
    spread_halo(padded_first, wide_first)
    write_ring(padded_second, swaps[1].receive(place))
    add_halo_terms(padded_second, weight_second, pre)
    for s in range(4):
        out, steep = gelu(pre[FLAT[s], :])
        value[FLAT[s], :] = out
        delta[WIDER[s], :] = rounded(grad[FLAT[s], :] * steep)
    swaps[2].send(halo_gradients(delta, turned_second), choose)

    spread_halo(padded_second, wide_second)
    weight_gradient(me, delta, delta_t, wide_second, second_sum)
    spread(delta, 1, wide_delta, 0, 50)
    second_sum.send_plane()
    field_gradient(wide_delta, turned_second, grad)
    add_strips(grad, swaps[2].receive(place))

    def backward_first(k, carry):
        error = rounded(grad[block(k), :] * slope[block(k), :])
        delta_view[pl.ds(2 + 8 * k, 8), pl.ds(8, S), :] = error.reshape(8, S, C)
        return carry

    lax.fori_loop(0, 6, backward_first, 0)
    weight_gradient(me, delta, delta_t, wide_first, first_sum)
    swaps[3].send(halo_gradients(delta, turned_first), choose)
    first_sum.send_plane()
    spread(delta, 1, wide_delta, 0, 50)
    field_gradient(wide_delta, turned_first, grad)
    second_sum.send_column()

    def store_out(k, carry):
        out_field[pl.ds(8 * k, 8)] = value[block(k), :].astype(bf16).reshape(8, S, C)
        return carry

    lax.fori_loop(0, 6, store_out, 0)
    first_sum.send_column()
    second_sum.send_whole()
    add_strips(grad, swaps[3].receive(place))

    def store_grad(k, carry):
        grad_fields[pl.ds(8 * k, 8)] = grad[block(k), :].astype(bf16).reshape(8, S, C)
        return carry

    lax.fori_loop(0, 6, store_grad, 0)
    first_sum.send_whole()
    second_sum.relay()
    second_sum.finish_own(second_out)
    second_sum.finish_other(second_out)
    first_sum.relay()
    first_sum.finish_own(first_out)
    first_sum.finish_other(first_out)
    for job in swaps + [first_sum, second_sum]:
        job.drain()


def store_kernel(*refs):
    copies = [
        pltpu.make_async_copy(refs[n], refs[4 + n], refs[8].at[n]) for n in range(4)
    ]
    for copy in copies:
        copy.start()
    for copy in copies:
        copy.wait()


def local(fields, weight_first, weight_second, neighbours, cotangent):
    vmem = pl.BlockSpec(memory_space=pltpu.VMEM)
    smem = pl.BlockSpec(memory_space=pltpu.SMEM)
    hbm = pl.BlockSpec(memory_space=pltpu.HBM)
    tile = (S, S, C)
    sums = (9, C, C)
    results = pl.pallas_call(
        step_kernel,
        out_shape=(
            pltpu.VMEM(tile, bf16),
            pltpu.VMEM(tile, bf16),
            pltpu.VMEM(sums, f32),
            pltpu.VMEM(sums, f32),
        ),
        in_specs=[hbm, hbm, hbm, smem, hbm],
        out_specs=(vmem, vmem, vmem, vmem),
        scratch_shapes=[
            pltpu.VMEM(tile, bf16),
            pltpu.VMEM(sums, bf16),
            pltpu.VMEM(sums, bf16),
            pltpu.VMEM(tile, bf16),
            pltpu.SemaphoreType.DMA((4,)),
            pltpu.VMEM((50 * PITCH, C), f32),
            pltpu.VMEM((50 * PITCH, C), f32),
            pltpu.VMEM((58 * PITCH, C), f32),
            pltpu.VMEM((50, S, 3 * C), bf16),
            pltpu.VMEM((50, S, 3 * C), bf16),
            pltpu.VMEM((50, S, 3 * C), bf16),
            pltpu.VMEM((C, S * S), bf16),
            pltpu.VMEM((S * S, C), f32),
            pltpu.VMEM((S * S, C), f32),
            pltpu.VMEM((S * S, C), f32),
            pltpu.VMEM((S * S, C), f32),
            pltpu.VMEM((C, 9 * C), bf16),
            pltpu.VMEM((C, 9 * C), bf16),
            pltpu.VMEM((4 * SLOT, 4 * SLOT), bf16),
            pltpu.VMEM((4 * SLOT, 4 * SLOT), bf16),
            pltpu.VMEM((4, 4, SLOT, C), bf16),
            pltpu.VMEM((4, 4, SLOT, C), bf16),
            pltpu.SemaphoreType.DMA((4, 2)),
            pltpu.VMEM(sums, f32),
            pltpu.VMEM(sums, f32),
        ]
        + REDUCE_SCRATCH
        + REDUCE_SCRATCH,
        compiler_params=pltpu.CompilerParams(
            collective_id=0, has_side_effects=True, vmem_limit_bytes=64_500_000
        ),
    )(
        fields.reshape(tile),
        weight_first.reshape(sums),
        weight_second.reshape(sums),
        neighbours.T,
        cotangent.reshape(tile),
    )
    out_field, grad_fields, first, second = pl.pallas_call(
        store_kernel,
        out_shape=(
            jax.ShapeDtypeStruct(tile, bf16),
            jax.ShapeDtypeStruct(tile, bf16),
            jax.ShapeDtypeStruct(sums, f32),
            jax.ShapeDtypeStruct(sums, f32),
        ),
        in_specs=[vmem, vmem, vmem, vmem],
        out_specs=(hbm, hbm, hbm, hbm),
        scratch_shapes=[pltpu.SemaphoreType.DMA((4,))],
        compiler_params=pltpu.CompilerParams(vmem_limit_bytes=1024 * 1024),
    )(*results)
    return (
        out_field[None, None],
        grad_fields[None, None],
        first.reshape(3, 3, C, C),
        second.reshape(3, 3, C, C),
    )


def solution(mesh):
    placed = (P("ens", "tile", None, None, None), P(), P(), P(), P("ens", "tile", None, None, None))
    return jax.shard_map(
        local,
        mesh=mesh,
        in_specs=placed,
        out_specs=(
            P("ens", "tile", None, None, None),
            P("ens", "tile", None, None, None),
            P(),
            P(),
        ),
        check_vma=False,
    )
```

```python
import jax
import jax.numpy as jnp
from jax import lax
from jax.experimental import pallas as pl
from jax.experimental.pallas import tpu as pltpu
from jax.sharding import PartitionSpec as P

MESH = pl.DeviceIdType.MESH
root_half = 0.7071067811865476
inv_root_tau = 0.3989422804014327
f32, bf16 = jnp.float32, jnp.bfloat16
S, C = 48, 128
PITCH = 64
SLOT = 64
OFFSETS = (1, -1, 16, -16)


TAPS = 5
FAR_FIRST = sorted(
    ((dx, dy) for dx in range(4) for dy in range(4) if dx or dy),
    key=lambda d: -(min(d[0], 4 - d[0]) + min(d[1], 4 - d[1])),
)


class Place:
    def __init__(self):
        ens = lax.axis_index("ens")
        tile = lax.axis_index("tile")
        self.tile = tile
        self.core = tile % 2
        self.z = ens * 4 + (tile // 2) % 4
        self.q = tile // 8

    def plane(self):
        x, y = self.q // 4, self.q % 4
        return [((x + dx) % 4) * 4 + (y + dy) % 4 for dx, dy in FAR_FIRST]

    def device(self, q, z, core):
        return {"ens": z // 4, "tile": q * 8 + (z % 4) * 2 + core}


def greet(me):
    barrier = pltpu.get_barrier_semaphore()

    def signal(target):
        pl.semaphore_signal(barrier, inc=1, device_id=target, device_id_type=MESH)

    for step in (1, -1):
        signal({"tile": (me.tile + step) % 128})
    for r in (4, 3, 5, 2, 6, 1, 7):
        signal(me.device(me.q, (me.z + r) % 8, me.core))
    for target in me.plane():
        signal(me.device(target, me.z, me.core))
    signal(me.device(me.q, me.z, 1 - me.core))
    return barrier


class Reduce:
    def __init__(self, me, grad, pair_out, pair_in, part, plane_in, column_in, whole, sems):
        self.me, self.grad = me, grad
        self.pair_out, self.pair_in, self.part = pair_out, pair_in, part
        self.plane_in, self.column_in, self.whole = plane_in, column_in, whole
        self.sems = sems

    def pair_copy(self, part, core):
        slots = pl.ds(2 * (1 - core), 3) if part == 0 else pl.ds(3 * core, 2)
        me = self.me
        return pltpu.make_async_remote_copy(
            src_ref=self.pair_out.at[slots],
            dst_ref=self.pair_in.at[slots],
            send_sem=self.sems.at[0, part],
            recv_sem=self.sems.at[1, part],
            device_id=me.device(me.q, me.z, 1 - me.core),
            device_id_type=MESH,
        )

    def plane_copy(self, target, source):
        return pltpu.make_async_remote_copy(
            src_ref=self.part.at[target],
            dst_ref=self.plane_in.at[source],
            send_sem=self.sems.at[0, 2],
            recv_sem=self.sems.at[1, 2],
            device_id=self.me.device(target, self.me.z, self.me.core),
            device_id_type=MESH,
        )

    def column_copy(self, target, source):
        return pltpu.make_async_remote_copy(
            src_ref=self.column_in.at[source],
            dst_ref=self.column_in.at[source],
            send_sem=self.sems.at[0, 3],
            recv_sem=self.sems.at[1, 3],
            device_id=self.me.device(self.me.q, target, self.me.core),
            device_id_type=MESH,
        )

    def whole_copy(self, target, source):
        core = self.me.core
        return pltpu.make_async_remote_copy(
            src_ref=self.whole.at[core, source],
            dst_ref=self.whole.at[core, source],
            send_sem=self.sems.at[0, 4],
            recv_sem=self.sems.at[1, 4],
            device_id=self.me.device(target, self.me.z, core),
            device_id_type=MESH,
        )

    def relay_copy(self, core):
        me = self.me
        return pltpu.make_async_remote_copy(
            src_ref=self.whole.at[core],
            dst_ref=self.whole.at[core],
            send_sem=self.sems.at[0, 5],
            recv_sem=self.sems.at[1, 5],
            device_id=me.device(me.q, me.z, 1 - me.core),
            device_id_type=MESH,
        )

    def stage(self, source, target, index):
        me = self.me
        return pltpu.make_async_remote_copy(
            src_ref=source,
            dst_ref=target,
            send_sem=self.sems.at[0, index],
            recv_sem=self.sems.at[1, index],
            device_id=me.device(me.q, me.z, 1 - me.core),
            device_id_type=MESH,
        )

    def plane_stage(self):
        return self.stage(self.part.at[pl.ds(0, 15)], self.plane_in.at[pl.ds(0, 15)], 2)

    def column_stage(self):
        return self.stage(self.column_in.at[pl.ds(0, 7)], self.column_in.at[pl.ds(0, 7)], 3)

    def whole_stage(self):
        blocks = self.whole.at[self.me.core, pl.ds(0, 15)]
        return self.stage(blocks, blocks, 4)

    def send_pair(self, part):
        core = self.me.core
        for u in range(3 - part):
            if part == 0:
                slot, tap = 2 * (1 - core) + u, 6 * (1 - core) + u
            else:
                slot, tap = 3 * core + u, 4 - core + u
            self.pair_out[slot] = self.grad[tap].astype(bf16)
        self.pair_copy(part, core).start()

    def send_plane(self):
        me = self.me
        for part in range(2):
            self.pair_copy(part, 1 - me.core).wait_recv()

        def band(m, carry):
            rows = pl.ds(pl.multiple_of(16 * m, 16), 16)
            for t in range(TAPS):
                total = self.grad[4 * me.core + t, rows, :] + self.pair_in[t, rows, :].astype(f32)
                self.part[2 * m, t] = total[:8].astype(bf16)
                self.part[2 * m + 1, t] = total[8:].astype(bf16)
            return carry

        lax.fori_loop(0, 8, band, 0)
        self.plane_in[me.q] = self.part[me.q]

        for target in me.plane():
            self.plane_copy(target, me.q).start()

    def send_column(self):
        me = self.me
        self.plane_stage().wait_recv()
        for t in range(TAPS):
            total = self.plane_in[0, t].astype(f32)
            for k in range(1, 16):
                total = total + self.plane_in[k, t].astype(f32)
            self.column_in[me.z, t] = total.astype(bf16)

        for r in (4, 3, 5, 2, 6, 1, 7):
            self.column_copy((me.z + r) % 8, me.z).start()

    def send_whole(self):
        me = self.me
        self.column_stage().wait_recv()
        for t in range(TAPS):
            total = self.column_in[0, t].astype(f32)
            for k in range(1, 8):
                total = total + self.column_in[k, t].astype(f32)
            self.whole[me.core, me.q, t] = total.astype(bf16)

        for target in me.plane():
            self.whole_copy(target, me.q).start()

    def relay(self):
        self.whole_stage().wait_recv()
        self.relay_copy(self.me.core).start()

    def finish(self, out, core):
        def body(k, carry):
            rows = pl.ds(pl.multiple_of(8 * k, 8), 8)
            for u in range(4):
                out[5 * core + u, rows, :] = self.whole[core, k, core + u].astype(f32)
            return carry

        lax.fori_loop(0, 16, body, 0, unroll=4)

    def finish_own(self, out):
        self.finish(out, self.me.core)

    def finish_other(self, out):
        me = self.me

        self.relay_copy(1 - me.core).wait_recv()
        self.finish(out, 1 - me.core)
        for k in range(16):
            out[4, 8 * k : 8 * k + 8, :] = self.whole[0, k, 4].astype(f32)

    def drain(self):
        me = self.me
        for part in range(2):
            self.pair_copy(part, me.core).wait_send()
        self.plane_stage().wait_send()
        self.column_stage().wait_send()
        self.whole_stage().wait_send()
        self.relay_copy(me.core).wait_send()


REDUCE_SCRATCH = [
    pltpu.VMEM((TAPS, 128, 128), bf16),
    pltpu.VMEM((TAPS, 128, 128), bf16),
    pltpu.VMEM((16, TAPS, 8, 128), bf16),
    pltpu.VMEM((16, TAPS, 8, 128), bf16),
    pltpu.VMEM((8, TAPS, 8, 128), bf16),
    pltpu.VMEM((2, 16, TAPS, 8, 128), bf16),
    pltpu.SemaphoreType.DMA((2, 6)),
]


class Swap:
    def __init__(self, me, outgoing, incoming, sems):
        self.me, self.outgoing, self.incoming, self.sems = me, outgoing, incoming, sems

    def copy(self, d):
        return pltpu.make_async_remote_copy(
            src_ref=self.outgoing.at[d, pl.ds(0, S)],
            dst_ref=self.incoming.at[d ^ 1, pl.ds(0, S)],
            send_sem=self.sems.at[0],
            recv_sem=self.sems.at[1],
            device_id={"tile": (self.me.tile + OFFSETS[d]) % 128},
            device_id_type=MESH,
        )

    def send(self, strips, choose):
        routed = jnp.dot(choose[...], strips, preferred_element_type=f32).astype(bf16)
        for d in range(4):
            self.outgoing[d] = routed[SLOT * d : SLOT * d + SLOT]
        for d in range(4):
            self.copy(d).start()

    def receive(self, place):
        self.everything().wait_recv()
        return jnp.dot(
            place[...], self.incoming[...].reshape(4 * SLOT, C), preferred_element_type=f32
        )

    def everything(self):
        return pltpu.make_async_remote_copy(
            src_ref=self.outgoing.at[:, pl.ds(0, S)],
            dst_ref=self.incoming.at[:, pl.ds(0, S)],
            send_sem=self.sems.at[0],
            recv_sem=self.sems.at[1],
            device_id={"tile": (self.me.tile + 1) % 128},
            device_id_type=MESH,
        )

    def drain(self):
        self.everything().wait_send()


def routing(me, neighbours, choose, place):
    sides = []
    for offset in OFFSETS:
        target = (me.tile + offset) % 128
        side = jnp.int32(0)
        for s in range(1, 4):
            side = side + jnp.where(neighbours[s, me.tile] == target, s, 0)
        sides.append(side)
    row = lax.broadcasted_iota(jnp.int32, (256, 256), 0)
    col = lax.broadcasted_iota(jnp.int32, (256, 256), 1)
    i, j = row % SLOT, col % SLOT
    inside = (i < S) & (j < S)
    same, flip = inside & (i == j), inside & (i + j == S - 1)

    def side_of(direction):
        out = jnp.full((256, 256), sides[0], jnp.int32)
        for d in range(1, 4):
            out = jnp.where(direction == d, sides[d], out)
        return out

    side = col // SLOT
    hit = (side_of(row // SLOT) == side) & (((side < 2) & same) | ((side >= 2) & flip))
    choose[...] = jnp.where(hit, 1.0, 0.0).astype(bf16)
    side = row // SLOT
    hit = (side_of(col // SLOT) == side) & (((side < 2) & flip) | ((side >= 2) & same))
    place[...] = jnp.where(hit, 1.0, 0.0).astype(bf16)


def pack_strips(strips):
    fill = jnp.zeros((SLOT - S, C), f32)
    return jnp.concatenate(
        [part for strip in strips for part in (strip, fill)], axis=0
    ).astype(bf16)


def border(base, pitch, left):
    start = base * pitch + left
    return (
        pl.ds(start, S),
        pl.ds(start + S - 1, S, stride=pitch),
        pl.ds(start + (S - 1) * pitch, S),
        pl.ds(start, S, stride=pitch),
    )


FLAT = border(0, S, 0)
PADDED = border(1, PITCH, 8)
WIDER = border(2, PITCH, 8)


def spread(padded, base, wide, first, count):
    view = padded.reshape(padded.shape[0] // PITCH, PITCH, C)

    def body(k, carry):
        r = first + k
        for b in range(3):
            wide[r, :, C * b : C * b + C] = view[r + base, pl.ds(7 + b, S), :].astype(bf16)
        return carry

    lax.fori_loop(0, count, body, 0, unroll=4)


def write_ring(padded, halo):
    top, right, bottom, left = (halo[SLOT * s : SLOT * s + S] for s in range(4))
    padded[pl.ds(PITCH + 7, S, stride=PITCH), :] = left
    padded[pl.ds(PITCH + 56, S, stride=PITCH), :] = right
    padded[pl.ds(8, S), :] = top
    padded[pl.ds(PITCH * 49 + 8, S), :] = bottom

    def corner(row, col, one, two):
        padded[pl.ds(PITCH * row + col, 1), :] = (0.5 * (one + two)).astype(bf16).astype(f32)

    corner(0, 7, top[:1], left[:1])
    corner(0, 56, top[S - 1 :], right[:1])
    corner(49, 7, left[S - 1 :], bottom[:1])
    corner(49, 56, bottom[S - 1 :], right[S - 1 :])


def add_halo_terms(padded, weight, pre):
    index = lax.broadcasted_iota(jnp.int32, (S, C), 0)

    def along_row(r):
        return [padded[pl.ds(PITCH * r + 7 + t, S), :] for t in range(3)]

    def along_column(col):
        lines = [padded[pl.ds(PITCH * t + col, S, stride=PITCH), :] for t in range(3)]
        lines[0] = jnp.where(index == 0, 0.0, lines[0])
        lines[2] = jnp.where(index == S - 1, 0.0, lines[2])
        return lines

    sides = (
        (along_row(0), (0, 1, 2)),
        (along_column(56), (2, 5, 8)),
        (along_row(49), (6, 7, 8)),
        (along_column(7), (0, 3, 6)),
    )
    terms = [
        jnp.dot(
            jnp.concatenate(lines, axis=1).astype(bf16),
            jnp.concatenate([weight[t] for t in taps], axis=0),
            preferred_element_type=f32,
        )
        for lines, taps in sides
    ]
    for where, term in zip(FLAT, terms):
        pre[where, :] += term


def spread_halo(padded, wide):
    view = padded.reshape(50, PITCH, C)
    for r in (0, 49):
        for b in range(3):
            wide[r, :, C * b : C * b + C] = view[r, pl.ds(7 + b, S), :].astype(bf16)

    def body(k, carry):
        r = 1 + k
        wide[r, :16, :C] = view[r, pl.ds(7, 16), :].astype(bf16)
        wide[r, 32:, 2 * C :] = view[r, pl.ds(41, 16), :].astype(bf16)
        return carry

    lax.fori_loop(0, S, body, 0, unroll=4)


def clear_ring(padded, rows, first):
    view = padded.reshape(padded.shape[0] // PITCH, PITCH, C)
    for r in rows:
        view[r] = jnp.zeros((PITCH, C), f32)
    view[first : first + S, :8, :] = jnp.zeros((S, 8, C), f32)
    view[first : first + S, 56:, :] = jnp.zeros((S, 8, C), f32)


def gelu(pre):
    below = 0.5 * (1.0 + lax.erf(pre * root_half))
    return pre * below, below + pre * jnp.exp(-0.5 * pre * pre) * inv_root_tau


def rounded(value):
    return value.astype(bf16).astype(f32)


def block(k):
    return pl.ds(pl.multiple_of(8 * S * k, 8 * S), 8 * S)


def taps_of(wide, start):
    return jnp.concatenate(
        [wide[pl.ds(start + a, 8)].reshape(8 * S, 3 * C) for a in range(3)], axis=1
    )


def dot_rows(rows, weight):
    return lax.dot_general(rows, weight, (((1,), (1,)), ((), ())), preferred_element_type=f32)


def halo_gradients(delta, turned):
    index = lax.broadcasted_iota(jnp.int32, (S, C), 0)

    def along_row(i):
        return [delta[pl.ds(PITCH * (i + 2) + 6 + t, 56), :] for t in range(3)]

    def along_column(j):
        return [delta[pl.ds(PITCH * t + 8 + j, 56, stride=PITCH), :] for t in range(3)]

    def tap(a, b):
        return turned[:, C * (3 * a + b) : C * (3 * a + b) + C]

    sides = (
        (along_row(0), [tap(2, t) for t in range(3)]),
        (along_column(S - 1), [tap(t, 0) for t in range(3)]),
        (along_row(S - 1), [tap(0, t) for t in range(3)]),
        (along_column(0), [tap(t, 2) for t in range(3)]),
    )
    parts = []
    for lines, blocks in sides:
        full = dot_rows(
            jnp.concatenate(lines, axis=1).astype(bf16), jnp.concatenate(blocks, axis=1)
        )
        strip = full[1 : S + 1]
        strip = strip + jnp.where(index == 0, 0.5 * full[:1], 0.0)
        strip = strip + jnp.where(index == S - 1, 0.5 * full[S + 1 : S + 2], 0.0)
        parts.append(strip)
    return pack_strips(parts)


def turn(weight, turned):
    for k in range(9):
        turned[:, C * k : C * k + C] = weight[8 - k]


def weight_gradient(me, delta, delta_t, wide, total):
    view = delta.reshape(delta.shape[0] // PITCH, PITCH, C)
    for k in range(6):
        rows = view[pl.ds(2 + 8 * k, 8), pl.ds(8, S), :].reshape(8 * S, C)
        delta_t[:, 8 * S * k : 8 * S * (k + 1)] = rows.T.astype(bf16)

    def tap_row(i):
        a = (1 - me.core) * (2 - i) + me.core * i
        flat = wide[pl.ds(a, S)].reshape(S * S, 3 * C)
        product = jnp.dot(delta_t[...], flat, preferred_element_type=f32)
        for b in range(3):
            total.grad[3 * a + b] = product[:, C * b : C * b + C].T

    for i in range(3):
        tap_row(i)
        if i < 2:
            total.send_pair(i)


def field_gradient(wide, turned, grad):
    def body(k, carry):
        grad[block(k), :] = dot_rows(taps_of(wide, 8 * k), turned[...])
        return carry

    lax.fori_loop(0, 6, body, 0)


def add_strips(grad, strips):
    for s in range(4):
        grad[FLAT[s], :] += strips[SLOT * s : SLOT * s + S]


def step_kernel(
    fields_hbm, weight_first_hbm, weight_second_hbm, neighbours, cotangent_hbm,
    out_field, grad_fields, first_out, second_out,
    fields, weight_first, weight_second, cotangent, load_sems,
    padded_first, padded_second, delta, wide_first, wide_second, wide_delta, delta_t,
    pre, slope, value, grad,
    turned_first, turned_second, choose, place, outgoing, incoming, swap_sems,
    grad_first, grad_second, *reduce_scratch,
):
    loads = [
        pltpu.make_async_copy(source, target, load_sems.at[n])
        for n, (source, target) in enumerate(
            (
                (fields_hbm, fields),
                (weight_first_hbm, weight_first),
                (weight_second_hbm, weight_second),
                (cotangent_hbm, cotangent),
            )
        )
    ]
    me = Place()
    barrier = greet(me)
    for load in loads:
        load.start()
    half = len(REDUCE_SCRATCH)
    second_sum = Reduce(me, grad_second, *reduce_scratch[:half])
    first_sum = Reduce(me, grad_first, *reduce_scratch[half:])
    swaps = [Swap(me, outgoing.at[e], incoming.at[e], swap_sems.at[e]) for e in range(4)]

    routing(me, neighbours, choose, place)
    incoming[:, :, S:, :] = jnp.zeros((4, 4, SLOT - S, C), bf16)
    clear_ring(padded_first, (0, 49), 1)
    clear_ring(padded_second, (0, 49), 1)
    clear_ring(delta, (0, 1, 50, 51, 52, 53, 54, 55, 56, 57), 2)
    first_view = padded_first.reshape(50, PITCH, C)
    second_view = padded_second.reshape(50, PITCH, C)
    delta_view = delta.reshape(58, PITCH, C)
    loads[0].wait()

    def load_fields(k, carry):
        first_view[pl.ds(1 + 8 * k, 8), pl.ds(8, S), :] = fields[pl.ds(8 * k, 8)].astype(f32)
        return carry

    lax.fori_loop(0, 6, load_fields, 0)
    strips = pack_strips([padded_first[where, :] for where in PADDED])
    pl.semaphore_wait(barrier, 25)
    swaps[0].send(strips, choose)

    spread(padded_first, 0, wide_first, 0, 50)
    loads[1].wait()

    def forward_first(k, carry):
        now = jnp.dot(
            taps_of(wide_first, 8 * k),
            weight_first[...].reshape(9 * C, C),
            preferred_element_type=f32,
        )
        pre[block(k), :] = now
        hidden, steep = gelu(now)
        slope[block(k), :] = steep
        second_view[pl.ds(1 + 8 * k, 8), pl.ds(8, S), :] = rounded(hidden).reshape(8, S, C)
        return carry

    lax.fori_loop(0, 6, forward_first, 0)
    write_ring(padded_first, swaps[0].receive(place))
    add_halo_terms(padded_first, weight_first, pre)
    strips = []
    for s in range(4):
        hidden, steep = gelu(pre[FLAT[s], :])
        hidden = rounded(hidden)
        slope[FLAT[s], :] = steep
        padded_second[PADDED[s], :] = hidden
        strips.append(hidden)
    swaps[1].send(pack_strips(strips), choose)

    spread(padded_second, 0, wide_second, 0, 50)
    loads[2].wait()
    loads[3].wait()

    def forward_second(k, carry):
        now = jnp.dot(
            taps_of(wide_second, 8 * k),
            weight_second[...].reshape(9 * C, C),
            preferred_element_type=f32,
        )
        pre[block(k), :] = now
        out, steep = gelu(now)
        value[block(k), :] = out
        cot = cotangent[pl.ds(8 * k, 8)].astype(f32)
        grad[block(k), :] = cot.reshape(8 * S, C)
        error = cot * steep.reshape(8, S, C)
        delta_view[pl.ds(2 + 8 * k, 8), pl.ds(8, S), :] = rounded(error)
        return carry

    lax.fori_loop(0, 6, forward_second, 0)
    turn(weight_second, turned_second)
    turn(weight_first, turned_first)
    spread_halo(padded_first, wide_first)
    write_ring(padded_second, swaps[1].receive(place))
    add_halo_terms(padded_second, weight_second, pre)
    for s in range(4):
        out, steep = gelu(pre[FLAT[s], :])
        value[FLAT[s], :] = out
        delta[WIDER[s], :] = rounded(grad[FLAT[s], :] * steep)
    swaps[2].send(halo_gradients(delta, turned_second), choose)

    spread_halo(padded_second, wide_second)
    weight_gradient(me, delta, delta_t, wide_second, second_sum)
    spread(delta, 1, wide_delta, 0, 50)
    second_sum.send_plane()
    field_gradient(wide_delta, turned_second, grad)
    add_strips(grad, swaps[2].receive(place))

    def backward_first(k, carry):
        error = rounded(grad[block(k), :] * slope[block(k), :])
        delta_view[pl.ds(2 + 8 * k, 8), pl.ds(8, S), :] = error.reshape(8, S, C)
        return carry

    lax.fori_loop(0, 6, backward_first, 0)
    weight_gradient(me, delta, delta_t, wide_first, first_sum)
    swaps[3].send(halo_gradients(delta, turned_first), choose)
    first_sum.send_plane()
    spread(delta, 1, wide_delta, 0, 50)
    field_gradient(wide_delta, turned_first, grad)
    second_sum.send_column()

    def store_out(k, carry):
        out_field[pl.ds(8 * k, 8)] = value[block(k), :].astype(bf16).reshape(8, S, C)
        return carry

    lax.fori_loop(0, 6, store_out, 0)
    first_sum.send_column()
    second_sum.send_whole()
    add_strips(grad, swaps[3].receive(place))

    def store_grad(k, carry):
        grad_fields[pl.ds(8 * k, 8)] = grad[block(k), :].astype(bf16).reshape(8, S, C)
        return carry

    lax.fori_loop(0, 6, store_grad, 0)
    first_sum.send_whole()
    second_sum.relay()
    second_sum.finish_own(second_out)
    second_sum.finish_other(second_out)
    first_sum.relay()
    first_sum.finish_own(first_out)
    first_sum.finish_other(first_out)
    for job in swaps + [first_sum, second_sum]:
        job.drain()


def store_kernel(*refs):
    copies = [
        pltpu.make_async_copy(refs[n], refs[4 + n], refs[8].at[n]) for n in range(4)
    ]
    for copy in copies:
        copy.start()
    for copy in copies:
        copy.wait()


def local(fields, weight_first, weight_second, neighbours, cotangent):
    vmem = pl.BlockSpec(memory_space=pltpu.VMEM)
    smem = pl.BlockSpec(memory_space=pltpu.SMEM)
    hbm = pl.BlockSpec(memory_space=pltpu.HBM)
    tile = (S, S, C)
    sums = (9, C, C)
    results = pl.pallas_call(
        step_kernel,
        out_shape=(
            pltpu.VMEM(tile, bf16),
            pltpu.VMEM(tile, bf16),
            pltpu.VMEM(sums, f32),
            pltpu.VMEM(sums, f32),
        ),
        in_specs=[hbm, hbm, hbm, smem, hbm],
        out_specs=(vmem, vmem, vmem, vmem),
        scratch_shapes=[
            pltpu.VMEM(tile, bf16),
            pltpu.VMEM(sums, bf16),
            pltpu.VMEM(sums, bf16),
            pltpu.VMEM(tile, bf16),
            pltpu.SemaphoreType.DMA((4,)),
            pltpu.VMEM((50 * PITCH, C), f32),
            pltpu.VMEM((50 * PITCH, C), f32),
            pltpu.VMEM((58 * PITCH, C), f32),
            pltpu.VMEM((50, S, 3 * C), bf16),
            pltpu.VMEM((50, S, 3 * C), bf16),
            pltpu.VMEM((50, S, 3 * C), bf16),
            pltpu.VMEM((C, S * S), bf16),
            pltpu.VMEM((S * S, C), f32),
            pltpu.VMEM((S * S, C), f32),
            pltpu.VMEM((S * S, C), f32),
            pltpu.VMEM((S * S, C), f32),
            pltpu.VMEM((C, 9 * C), bf16),
            pltpu.VMEM((C, 9 * C), bf16),
            pltpu.VMEM((4 * SLOT, 4 * SLOT), bf16),
            pltpu.VMEM((4 * SLOT, 4 * SLOT), bf16),
            pltpu.VMEM((4, 4, SLOT, C), bf16),
            pltpu.VMEM((4, 4, SLOT, C), bf16),
            pltpu.SemaphoreType.DMA((4, 2)),
            pltpu.VMEM(sums, f32),
            pltpu.VMEM(sums, f32),
        ]
        + REDUCE_SCRATCH
        + REDUCE_SCRATCH,
        compiler_params=pltpu.CompilerParams(
            collective_id=0, has_side_effects=True, vmem_limit_bytes=64_500_000
        ),
    )(
        fields.reshape(tile),
        weight_first.reshape(sums),
        weight_second.reshape(sums),
        neighbours.T,
        cotangent.reshape(tile),
    )
    out_field, grad_fields, first, second = pl.pallas_call(
        store_kernel,
        out_shape=(
            jax.ShapeDtypeStruct(tile, bf16),
            jax.ShapeDtypeStruct(tile, bf16),
            jax.ShapeDtypeStruct(sums, f32),
            jax.ShapeDtypeStruct(sums, f32),
        ),
        in_specs=[vmem, vmem, vmem, vmem],
        out_specs=(hbm, hbm, hbm, hbm),
        scratch_shapes=[pltpu.SemaphoreType.DMA((4,))],
        compiler_params=pltpu.CompilerParams(vmem_limit_bytes=1024 * 1024),
    )(*results)
    return (
        out_field[None, None],
        grad_fields[None, None],
        first.reshape(3, 3, C, C),
        second.reshape(3, 3, C, C),
    )


def solution(mesh):
    placed = (P("ens", "tile", None, None, None), P(), P(), P(), P("ens", "tile", None, None, None))
    return jax.shard_map(
        local,
        mesh=mesh,
        in_specs=placed,
        out_specs=(
            P("ens", "tile", None, None, None),
            P("ens", "tile", None, None, None),
            P(),
            P(),
        ),
        check_vma=False,
    )
```

```python
import jax
import jax.numpy as jnp
from jax import lax
from jax.experimental import pallas as pl
from jax.experimental.pallas import tpu as pltpu
from jax.sharding import PartitionSpec as P

MESH = pl.DeviceIdType.MESH
root_half = 0.7071067811865476
inv_root_tau = 0.3989422804014327
f32, bf16 = jnp.float32, jnp.bfloat16
S, C = 48, 128
PITCH = 64
SLOT = 64
OFFSETS = (1, -1, 16, -16)


TAPS = 5
FAR = 5
FAR_FIRST = sorted(
    ((dx, dy) for dx in range(4) for dy in range(4) if dx or dy),
    key=lambda d: -(min(d[0], 4 - d[0]) + min(d[1], 4 - d[1])),
)


class Place:
    def __init__(self):
        ens = lax.axis_index("ens")
        tile = lax.axis_index("tile")
        self.tile = tile
        self.core = tile % 2
        self.z = ens * 4 + (tile // 2) % 4
        self.q = tile // 8

    def plane(self):
        x, y = self.q // 4, self.q % 4
        return [((x + dx) % 4) * 4 + (y + dy) % 4 for dx, dy in FAR_FIRST]

    def device(self, q, z, core):
        return {"ens": z // 4, "tile": q * 8 + (z % 4) * 2 + core}


def greet(me):
    barrier = pltpu.get_barrier_semaphore()

    def signal(target):
        pl.semaphore_signal(barrier, inc=1, device_id=target, device_id_type=MESH)

    for step in (1, -1):
        signal({"tile": (me.tile + step) % 128})
    for r in (4, 3, 5, 2, 6, 1, 7):
        signal(me.device(me.q, (me.z + r) % 8, me.core))
    for target in me.plane():
        signal(me.device(target, me.z, me.core))
    for target in me.plane()[:FAR]:
        signal(me.device(target, me.z, 1 - me.core))
    signal(me.device(me.q, me.z, 1 - me.core))
    return barrier


class Reduce:
    def __init__(self, me, grad, pair_out, pair_in, part, plane_in, column_in, whole, sems):
        self.me, self.grad = me, grad
        self.pair_out, self.pair_in, self.part = pair_out, pair_in, part
        self.plane_in, self.column_in, self.whole = plane_in, column_in, whole
        self.sems = sems

    def pair_copy(self, part, core):
        slots = pl.ds(2 * (1 - core), 3) if part == 0 else pl.ds(3 * core, 2)
        me = self.me
        return pltpu.make_async_remote_copy(
            src_ref=self.pair_out.at[slots],
            dst_ref=self.pair_in.at[slots],
            send_sem=self.sems.at[0, part],
            recv_sem=self.sems.at[1, part],
            device_id=me.device(me.q, me.z, 1 - me.core),
            device_id_type=MESH,
        )

    def plane_copy(self, target, source):
        return pltpu.make_async_remote_copy(
            src_ref=self.part.at[target],
            dst_ref=self.plane_in.at[source],
            send_sem=self.sems.at[0, 2],
            recv_sem=self.sems.at[1, 2],
            device_id=self.me.device(target, self.me.z, self.me.core),
            device_id_type=MESH,
        )

    def column_copy(self, target, source):
        return pltpu.make_async_remote_copy(
            src_ref=self.column_in.at[source],
            dst_ref=self.column_in.at[source],
            send_sem=self.sems.at[0, 3],
            recv_sem=self.sems.at[1, 3],
            device_id=self.me.device(self.me.q, target, self.me.core),
            device_id_type=MESH,
        )

    def whole_copy(self, target, target_core, index):
        me = self.me
        return pltpu.make_async_remote_copy(
            src_ref=self.whole.at[me.core, me.q],
            dst_ref=self.whole.at[me.core, me.q],
            send_sem=self.sems.at[0, index],
            recv_sem=self.sems.at[1, index],
            device_id=me.device(target, me.z, target_core),
            device_id_type=MESH,
        )

    def relay_copy(self, source):
        block = self.whole.at[self.me.core, source]
        return self.stage(block, block, 5)

    def stage(self, source, target, index):
        me = self.me
        return pltpu.make_async_remote_copy(
            src_ref=source,
            dst_ref=target,
            send_sem=self.sems.at[0, index],
            recv_sem=self.sems.at[1, index],
            device_id=me.device(me.q, me.z, 1 - me.core),
            device_id_type=MESH,
        )

    def plane_stage(self):
        return self.stage(self.part.at[pl.ds(0, 15)], self.plane_in.at[pl.ds(0, 15)], 2)

    def column_stage(self):
        return self.stage(self.column_in.at[pl.ds(0, 7)], self.column_in.at[pl.ds(0, 7)], 3)

    def whole_stage(self, index, count):
        blocks = self.whole.at[0, pl.ds(0, count)]
        return self.stage(blocks, blocks, index)

    def send_pair(self, part):
        core = self.me.core
        for u in range(3 - part):
            if part == 0:
                slot, tap = 2 * (1 - core) + u, 6 * (1 - core) + u
            else:
                slot, tap = 3 * core + u, 4 - core + u
            self.pair_out[slot] = self.grad[tap].astype(bf16)
        self.pair_copy(part, core).start()

    def send_plane(self):
        me = self.me
        for part in range(2):
            self.pair_copy(part, 1 - me.core).wait_recv()

        def band(m, carry):
            rows = pl.ds(pl.multiple_of(16 * m, 16), 16)
            for t in range(TAPS):
                total = self.grad[4 * me.core + t, rows, :] + self.pair_in[t, rows, :].astype(f32)
                self.part[2 * m, t] = total[:8].astype(bf16)
                self.part[2 * m + 1, t] = total[8:].astype(bf16)
            return carry

        lax.fori_loop(0, 8, band, 0)
        self.plane_in[me.q] = self.part[me.q]

        for target in me.plane():
            self.plane_copy(target, me.q).start()

    def send_column(self):
        me = self.me
        self.plane_stage().wait_recv()
        for t in range(TAPS):
            total = self.plane_in[0, t].astype(f32)
            for k in range(1, 16):
                total = total + self.plane_in[k, t].astype(f32)
            self.column_in[me.z, t] = total.astype(bf16)

        for r in (4, 3, 5, 2, 6, 1, 7):
            self.column_copy((me.z + r) % 8, me.z).start()

    def send_whole(self):
        me = self.me
        self.column_stage().wait_recv()
        for t in range(TAPS):
            total = self.column_in[0, t].astype(f32)
            for k in range(1, 8):
                total = total + self.column_in[k, t].astype(f32)
            self.whole[me.core, me.q, t] = total.astype(bf16)

        for n, target in enumerate(me.plane()):
            self.whole_copy(target, me.core, 4 if n < FAR else 7).start()
            if n < FAR:
                self.whole_copy(target, 1 - me.core, 6).start()
        self.relay_copy(me.q).start()

    def relay(self):
        self.whole_stage(7, 15 - FAR).wait_recv()
        for source in self.me.plane()[FAR:]:
            self.relay_copy(source).start()
        self.whole_stage(4, FAR).wait_recv()

    def finish(self, out, core):
        def body(k, carry):
            rows = pl.ds(pl.multiple_of(8 * k, 8), 8)
            for u in range(4):
                out[5 * core + u, rows, :] = self.whole[core, k, core + u].astype(f32)
            return carry

        lax.fori_loop(0, 16, body, 0, unroll=4)

    def finish_own(self, out):
        self.finish(out, self.me.core)

    def finish_other(self, out):
        me = self.me

        self.whole_stage(6, FAR).wait_recv()
        self.whole_stage(5, 16 - FAR).wait_recv()
        self.finish(out, 1 - me.core)
        for k in range(16):
            out[4, 8 * k : 8 * k + 8, :] = self.whole[0, k, 4].astype(f32)

    def drain(self):
        me = self.me
        for part in range(2):
            self.pair_copy(part, me.core).wait_send()
        self.plane_stage().wait_send()
        self.column_stage().wait_send()
        for index, count in ((4, FAR), (5, 16 - FAR), (6, FAR), (7, 15 - FAR)):
            self.whole_stage(index, count).wait_send()


REDUCE_SCRATCH = [
    pltpu.VMEM((TAPS, 128, 128), bf16),
    pltpu.VMEM((TAPS, 128, 128), bf16),
    pltpu.VMEM((16, TAPS, 8, 128), bf16),
    pltpu.VMEM((16, TAPS, 8, 128), bf16),
    pltpu.VMEM((8, TAPS, 8, 128), bf16),
    pltpu.VMEM((2, 16, TAPS, 8, 128), bf16),
    pltpu.SemaphoreType.DMA((2, 8)),
]


class Swap:
    def __init__(self, me, outgoing, incoming, sems):
        self.me, self.outgoing, self.incoming, self.sems = me, outgoing, incoming, sems

    def copy(self, d):
        return pltpu.make_async_remote_copy(
            src_ref=self.outgoing.at[d, pl.ds(0, S)],
            dst_ref=self.incoming.at[d ^ 1, pl.ds(0, S)],
            send_sem=self.sems.at[0],
            recv_sem=self.sems.at[1],
            device_id={"tile": (self.me.tile + OFFSETS[d]) % 128},
            device_id_type=MESH,
        )

    def send(self, strips, choose):
        routed = jnp.dot(choose[...], strips, preferred_element_type=f32).astype(bf16)
        for d in range(4):
            self.outgoing[d] = routed[SLOT * d : SLOT * d + SLOT]
        for d in range(4):
            self.copy(d).start()

    def receive(self, place):
        self.everything().wait_recv()
        return jnp.dot(
            place[...], self.incoming[...].reshape(4 * SLOT, C), preferred_element_type=f32
        )

    def everything(self):
        return pltpu.make_async_remote_copy(
            src_ref=self.outgoing.at[:, pl.ds(0, S)],
            dst_ref=self.incoming.at[:, pl.ds(0, S)],
            send_sem=self.sems.at[0],
            recv_sem=self.sems.at[1],
            device_id={"tile": (self.me.tile + 1) % 128},
            device_id_type=MESH,
        )

    def drain(self):
        self.everything().wait_send()


def routing(me, neighbours, choose, place):
    sides = []
    for offset in OFFSETS:
        target = (me.tile + offset) % 128
        side = jnp.int32(0)
        for s in range(1, 4):
            side = side + jnp.where(neighbours[s, me.tile] == target, s, 0)
        sides.append(side)
    row = lax.broadcasted_iota(jnp.int32, (256, 256), 0)
    col = lax.broadcasted_iota(jnp.int32, (256, 256), 1)
    i, j = row % SLOT, col % SLOT
    inside = (i < S) & (j < S)
    same, flip = inside & (i == j), inside & (i + j == S - 1)

    def side_of(direction):
        out = jnp.full((256, 256), sides[0], jnp.int32)
        for d in range(1, 4):
            out = jnp.where(direction == d, sides[d], out)
        return out

    side = col // SLOT
    hit = (side_of(row // SLOT) == side) & (((side < 2) & same) | ((side >= 2) & flip))
    choose[...] = jnp.where(hit, 1.0, 0.0).astype(bf16)
    side = row // SLOT
    hit = (side_of(col // SLOT) == side) & (((side < 2) & flip) | ((side >= 2) & same))
    place[...] = jnp.where(hit, 1.0, 0.0).astype(bf16)


def pack_strips(strips):
    fill = jnp.zeros((SLOT - S, C), f32)
    return jnp.concatenate(
        [part for strip in strips for part in (strip, fill)], axis=0
    ).astype(bf16)


def border(base, pitch, left):
    start = base * pitch + left
    return (
        pl.ds(start, S),
        pl.ds(start + S - 1, S, stride=pitch),
        pl.ds(start + (S - 1) * pitch, S),
        pl.ds(start, S, stride=pitch),
    )


FLAT = border(0, S, 0)
PADDED = border(1, PITCH, 8)
WIDER = border(2, PITCH, 8)


def spread(padded, base, wide, first, count):
    view = padded.reshape(padded.shape[0] // PITCH, PITCH, C)

    def body(k, carry):
        r = first + k
        for b in range(3):
            wide[r, :, C * b : C * b + C] = view[r + base, pl.ds(7 + b, S), :].astype(bf16)
        return carry

    lax.fori_loop(0, count, body, 0, unroll=4)


def write_ring(padded, halo):
    top, right, bottom, left = (halo[SLOT * s : SLOT * s + S] for s in range(4))
    padded[pl.ds(PITCH + 7, S, stride=PITCH), :] = left
    padded[pl.ds(PITCH + 56, S, stride=PITCH), :] = right
    padded[pl.ds(8, S), :] = top
    padded[pl.ds(PITCH * 49 + 8, S), :] = bottom

    def corner(row, col, one, two):
        padded[pl.ds(PITCH * row + col, 1), :] = (0.5 * (one + two)).astype(bf16).astype(f32)

    corner(0, 7, top[:1], left[:1])
    corner(0, 56, top[S - 1 :], right[:1])
    corner(49, 7, left[S - 1 :], bottom[:1])
    corner(49, 56, bottom[S - 1 :], right[S - 1 :])


def add_halo_terms(padded, weight, pre):
    index = lax.broadcasted_iota(jnp.int32, (S, C), 0)

    def along_row(r):
        return [padded[pl.ds(PITCH * r + 7 + t, S), :] for t in range(3)]

    def along_column(col):
        lines = [padded[pl.ds(PITCH * t + col, S, stride=PITCH), :] for t in range(3)]
        lines[0] = jnp.where(index == 0, 0.0, lines[0])
        lines[2] = jnp.where(index == S - 1, 0.0, lines[2])
        return lines

    sides = (
        (along_row(0), (0, 1, 2)),
        (along_column(56), (2, 5, 8)),
        (along_row(49), (6, 7, 8)),
        (along_column(7), (0, 3, 6)),
    )
    terms = [
        jnp.dot(
            jnp.concatenate(lines, axis=1).astype(bf16),
            jnp.concatenate([weight[t] for t in taps], axis=0),
            preferred_element_type=f32,
        )
        for lines, taps in sides
    ]
    for where, term in zip(FLAT, terms):
        pre[where, :] += term


def spread_halo(padded, wide):
    view = padded.reshape(50, PITCH, C)
    for r in (0, 49):
        for b in range(3):
            wide[r, :, C * b : C * b + C] = view[r, pl.ds(7 + b, S), :].astype(bf16)

    def body(k, carry):
        r = 1 + k
        wide[r, :16, :C] = view[r, pl.ds(7, 16), :].astype(bf16)
        wide[r, 32:, 2 * C :] = view[r, pl.ds(41, 16), :].astype(bf16)
        return carry

    lax.fori_loop(0, S, body, 0, unroll=4)


def clear_ring(padded, rows, first):
    view = padded.reshape(padded.shape[0] // PITCH, PITCH, C)
    for r in rows:
        view[r] = jnp.zeros((PITCH, C), f32)
    view[first : first + S, :8, :] = jnp.zeros((S, 8, C), f32)
    view[first : first + S, 56:, :] = jnp.zeros((S, 8, C), f32)


def gelu(pre):
    below = 0.5 * (1.0 + lax.erf(pre * root_half))
    return pre * below, below + pre * jnp.exp(-0.5 * pre * pre) * inv_root_tau


def rounded(value):
    return value.astype(bf16).astype(f32)


def block(k):
    return pl.ds(pl.multiple_of(8 * S * k, 8 * S), 8 * S)


def taps_of(wide, start):
    return jnp.concatenate(
        [wide[pl.ds(start + a, 8)].reshape(8 * S, 3 * C) for a in range(3)], axis=1
    )


def dot_rows(rows, weight):
    return lax.dot_general(rows, weight, (((1,), (1,)), ((), ())), preferred_element_type=f32)


def halo_gradients(delta, turned):
    index = lax.broadcasted_iota(jnp.int32, (S, C), 0)

    def along_row(i):
        return [delta[pl.ds(PITCH * (i + 2) + 6 + t, 56), :] for t in range(3)]

    def along_column(j):
        return [delta[pl.ds(PITCH * t + 8 + j, 56, stride=PITCH), :] for t in range(3)]

    def tap(a, b):
        return turned[:, C * (3 * a + b) : C * (3 * a + b) + C]

    sides = (
        (along_row(0), [tap(2, t) for t in range(3)]),
        (along_column(S - 1), [tap(t, 0) for t in range(3)]),
        (along_row(S - 1), [tap(0, t) for t in range(3)]),
        (along_column(0), [tap(t, 2) for t in range(3)]),
    )
    parts = []
    for lines, blocks in sides:
        full = dot_rows(
            jnp.concatenate(lines, axis=1).astype(bf16), jnp.concatenate(blocks, axis=1)
        )
        strip = full[1 : S + 1]
        strip = strip + jnp.where(index == 0, 0.5 * full[:1], 0.0)
        strip = strip + jnp.where(index == S - 1, 0.5 * full[S + 1 : S + 2], 0.0)
        parts.append(strip)
    return pack_strips(parts)


def turn(weight, turned):
    for k in range(9):
        turned[:, C * k : C * k + C] = weight[8 - k]


def weight_gradient(me, delta, delta_t, wide, total):
    view = delta.reshape(delta.shape[0] // PITCH, PITCH, C)
    for k in range(6):
        rows = view[pl.ds(2 + 8 * k, 8), pl.ds(8, S), :].reshape(8 * S, C)
        delta_t[:, 8 * S * k : 8 * S * (k + 1)] = rows.T.astype(bf16)

    def tap_row(i):
        a = (1 - me.core) * (2 - i) + me.core * i
        flat = wide[pl.ds(a, S)].reshape(S * S, 3 * C)
        product = jnp.dot(delta_t[...], flat, preferred_element_type=f32)
        for b in range(3):
            total.grad[3 * a + b] = product[:, C * b : C * b + C].T

    for i in range(3):
        tap_row(i)
        if i < 2:
            total.send_pair(i)


def field_gradient(wide, turned, grad):
    def body(k, carry):
        grad[block(k), :] = dot_rows(taps_of(wide, 8 * k), turned[...])
        return carry

    lax.fori_loop(0, 6, body, 0)


def add_strips(grad, strips):
    for s in range(4):
        grad[FLAT[s], :] += strips[SLOT * s : SLOT * s + S]


def step_kernel(
    fields_hbm, weight_first_hbm, weight_second_hbm, neighbours, cotangent_hbm,
    out_field, grad_fields, first_out, second_out,
    fields, weight_first, weight_second, cotangent, load_sems,
    padded_first, padded_second, delta, wide_first, wide_second, wide_delta, delta_t,
    pre, slope, value, grad,
    turned_first, turned_second, choose, place, outgoing, incoming, swap_sems,
    grad_first, grad_second, *reduce_scratch,
):
    loads = [
        pltpu.make_async_copy(source, target, load_sems.at[n])
        for n, (source, target) in enumerate(
            (
                (fields_hbm, fields),
                (weight_first_hbm, weight_first),
                (weight_second_hbm, weight_second),
                (cotangent_hbm, cotangent),
            )
        )
    ]
    me = Place()
    barrier = greet(me)
    for load in loads:
        load.start()
    half = len(REDUCE_SCRATCH)
    second_sum = Reduce(me, grad_second, *reduce_scratch[:half])
    first_sum = Reduce(me, grad_first, *reduce_scratch[half:])
    swaps = [Swap(me, outgoing.at[e], incoming.at[e], swap_sems.at[e]) for e in range(4)]

    routing(me, neighbours, choose, place)
    incoming[:, :, S:, :] = jnp.zeros((4, 4, SLOT - S, C), bf16)
    clear_ring(padded_first, (0, 49), 1)
    clear_ring(padded_second, (0, 49), 1)
    clear_ring(delta, (0, 1, 50, 51, 52, 53, 54, 55, 56, 57), 2)
    first_view = padded_first.reshape(50, PITCH, C)
    second_view = padded_second.reshape(50, PITCH, C)
    delta_view = delta.reshape(58, PITCH, C)
    loads[0].wait()

    def load_fields(k, carry):
        first_view[pl.ds(1 + 8 * k, 8), pl.ds(8, S), :] = fields[pl.ds(8 * k, 8)].astype(f32)
        return carry

    lax.fori_loop(0, 6, load_fields, 0)
    strips = pack_strips([padded_first[where, :] for where in PADDED])
    pl.semaphore_wait(barrier, 25 + FAR)
    swaps[0].send(strips, choose)

    spread(padded_first, 0, wide_first, 0, 50)
    loads[1].wait()

    def forward_first(k, carry):
        now = jnp.dot(
            taps_of(wide_first, 8 * k),
            weight_first[...].reshape(9 * C, C),
            preferred_element_type=f32,
        )
        pre[block(k), :] = now
        hidden, steep = gelu(now)
        slope[block(k), :] = steep
        second_view[pl.ds(1 + 8 * k, 8), pl.ds(8, S), :] = rounded(hidden).reshape(8, S, C)
        return carry

    lax.fori_loop(0, 6, forward_first, 0)
    write_ring(padded_first, swaps[0].receive(place))
    add_halo_terms(padded_first, weight_first, pre)
    strips = []
    for s in range(4):
        hidden, steep = gelu(pre[FLAT[s], :])
        hidden = rounded(hidden)
        slope[FLAT[s], :] = steep
        padded_second[PADDED[s], :] = hidden
        strips.append(hidden)
    swaps[1].send(pack_strips(strips), choose)

    spread(padded_second, 0, wide_second, 0, 50)
    loads[2].wait()
    loads[3].wait()

    def forward_second(k, carry):
        now = jnp.dot(
            taps_of(wide_second, 8 * k),
            weight_second[...].reshape(9 * C, C),
            preferred_element_type=f32,
        )
        pre[block(k), :] = now
        out, steep = gelu(now)
        value[block(k), :] = out
        cot = cotangent[pl.ds(8 * k, 8)].astype(f32)
        grad[block(k), :] = cot.reshape(8 * S, C)
        error = cot * steep.reshape(8, S, C)
        delta_view[pl.ds(2 + 8 * k, 8), pl.ds(8, S), :] = rounded(error)
        return carry

    lax.fori_loop(0, 6, forward_second, 0)
    turn(weight_second, turned_second)
    turn(weight_first, turned_first)
    spread_halo(padded_first, wide_first)
    write_ring(padded_second, swaps[1].receive(place))
    add_halo_terms(padded_second, weight_second, pre)
    for s in range(4):
        out, steep = gelu(pre[FLAT[s], :])
        value[FLAT[s], :] = out
        delta[WIDER[s], :] = rounded(grad[FLAT[s], :] * steep)
    swaps[2].send(halo_gradients(delta, turned_second), choose)

    spread_halo(padded_second, wide_second)
    weight_gradient(me, delta, delta_t, wide_second, second_sum)
    spread(delta, 1, wide_delta, 0, 50)
    second_sum.send_plane()
    field_gradient(wide_delta, turned_second, grad)
    add_strips(grad, swaps[2].receive(place))

    def backward_first(k, carry):
        error = rounded(grad[block(k), :] * slope[block(k), :])
        delta_view[pl.ds(2 + 8 * k, 8), pl.ds(8, S), :] = error.reshape(8, S, C)
        return carry

    lax.fori_loop(0, 6, backward_first, 0)
    weight_gradient(me, delta, delta_t, wide_first, first_sum)
    swaps[3].send(halo_gradients(delta, turned_first), choose)
    first_sum.send_plane()
    spread(delta, 1, wide_delta, 0, 50)
    field_gradient(wide_delta, turned_first, grad)
    second_sum.send_column()

    def store_out(k, carry):
        out_field[pl.ds(8 * k, 8)] = value[block(k), :].astype(bf16).reshape(8, S, C)
        return carry

    lax.fori_loop(0, 6, store_out, 0)
    first_sum.send_column()
    second_sum.send_whole()
    add_strips(grad, swaps[3].receive(place))

    def store_grad(k, carry):
        grad_fields[pl.ds(8 * k, 8)] = grad[block(k), :].astype(bf16).reshape(8, S, C)
        return carry

    lax.fori_loop(0, 6, store_grad, 0)
    first_sum.send_whole()
    second_sum.relay()
    second_sum.finish_own(second_out)
    second_sum.finish_other(second_out)
    first_sum.relay()
    first_sum.finish_own(first_out)
    first_sum.finish_other(first_out)
    for job in swaps + [first_sum, second_sum]:
        job.drain()


def store_kernel(*refs):
    copies = [
        pltpu.make_async_copy(refs[n], refs[4 + n], refs[8].at[n]) for n in range(4)
    ]
    for copy in copies:
        copy.start()
    for copy in copies:
        copy.wait()


def local(fields, weight_first, weight_second, neighbours, cotangent):
    vmem = pl.BlockSpec(memory_space=pltpu.VMEM)
    smem = pl.BlockSpec(memory_space=pltpu.SMEM)
    hbm = pl.BlockSpec(memory_space=pltpu.HBM)
    tile = (S, S, C)
    sums = (9, C, C)
    results = pl.pallas_call(
        step_kernel,
        out_shape=(
            pltpu.VMEM(tile, bf16),
            pltpu.VMEM(tile, bf16),
            pltpu.VMEM(sums, f32),
            pltpu.VMEM(sums, f32),
        ),
        in_specs=[hbm, hbm, hbm, smem, hbm],
        out_specs=(vmem, vmem, vmem, vmem),
        scratch_shapes=[
            pltpu.VMEM(tile, bf16),
            pltpu.VMEM(sums, bf16),
            pltpu.VMEM(sums, bf16),
            pltpu.VMEM(tile, bf16),
            pltpu.SemaphoreType.DMA((4,)),
            pltpu.VMEM((50 * PITCH, C), f32),
            pltpu.VMEM((50 * PITCH, C), f32),
            pltpu.VMEM((58 * PITCH, C), f32),
            pltpu.VMEM((50, S, 3 * C), bf16),
            pltpu.VMEM((50, S, 3 * C), bf16),
            pltpu.VMEM((50, S, 3 * C), bf16),
            pltpu.VMEM((C, S * S), bf16),
            pltpu.VMEM((S * S, C), f32),
            pltpu.VMEM((S * S, C), f32),
            pltpu.VMEM((S * S, C), f32),
            pltpu.VMEM((S * S, C), f32),
            pltpu.VMEM((C, 9 * C), bf16),
            pltpu.VMEM((C, 9 * C), bf16),
            pltpu.VMEM((4 * SLOT, 4 * SLOT), bf16),
            pltpu.VMEM((4 * SLOT, 4 * SLOT), bf16),
            pltpu.VMEM((4, 4, SLOT, C), bf16),
            pltpu.VMEM((4, 4, SLOT, C), bf16),
            pltpu.SemaphoreType.DMA((4, 2)),
            pltpu.VMEM(sums, f32),
            pltpu.VMEM(sums, f32),
        ]
        + REDUCE_SCRATCH
        + REDUCE_SCRATCH,
        compiler_params=pltpu.CompilerParams(
            collective_id=0, has_side_effects=True, vmem_limit_bytes=64_500_000
        ),
    )(
        fields.reshape(tile),
        weight_first.reshape(sums),
        weight_second.reshape(sums),
        neighbours.T,
        cotangent.reshape(tile),
    )
    out_field, grad_fields, first, second = pl.pallas_call(
        store_kernel,
        out_shape=(
            jax.ShapeDtypeStruct(tile, bf16),
            jax.ShapeDtypeStruct(tile, bf16),
            jax.ShapeDtypeStruct(sums, f32),
            jax.ShapeDtypeStruct(sums, f32),
        ),
        in_specs=[vmem, vmem, vmem, vmem],
        out_specs=(hbm, hbm, hbm, hbm),
        scratch_shapes=[pltpu.SemaphoreType.DMA((4,))],
        compiler_params=pltpu.CompilerParams(vmem_limit_bytes=1024 * 1024),
    )(*results)
    return (
        out_field[None, None],
        grad_fields[None, None],
        first.reshape(3, 3, C, C),
        second.reshape(3, 3, C, C),
    )


def solution(mesh):
    placed = (P("ens", "tile", None, None, None), P(), P(), P(), P("ens", "tile", None, None, None))
    return jax.shard_map(
        local,
        mesh=mesh,
        in_specs=placed,
        out_specs=(
            P("ens", "tile", None, None, None),
            P("ens", "tile", None, None, None),
            P(),
            P(),
        ),
        check_vma=False,
    )
```
